32 devices in a mesh: noise: 8 (over z, y), tile: 4 (over x, core).
Axes of the slice: x: 2, y: 2, z: 4, core: 2. Of those that a mesh axis runs over, the one named last changes fastest.
Arguments:
- queue_state: float32 [32, 69, 4, 256], P('noise', None, 'tile'), may hold values from -6 to 6
- fresh_noise: float32 [2, 69, 4, 256], P(None, None, 'tile'), may hold values from -6 to 6
- plan: float32 [17], replicated, may hold values from 0.5 to 2
- levels: int32 [32], P('noise'), may hold values from 0 to 15
- neighbours: int32 [4, 4], replicated, may hold values from -1 to 3, as said below
- in_weight: bfloat16 [256, 69], replicated, may hold values from -0.75 to 0.75
- level_embed: float32 [256], replicated, may hold values from -3 to 3
- conv_weight: bfloat16 [9, 256, 256], replicated, may hold values from -0.125 to 0.125
- norm_gain: float32 [256], replicated, may hold values from 0.5 to 1.5
- query_weight: bfloat16 [256, 256], replicated, may hold values from -0.375 to 0.375
- memory_weight: bfloat16 [512, 256], replicated, may hold values from -0.375 to 0.375
- attend_out: bfloat16 [256, 256], replicated, may hold values from -0.375 to 0.375
- decode_weight: bfloat16 [69, 256], replicated, may hold values from -0.375 to 0.375
Outputs:
- queue_after: float32 [32, 69, 4, 256], P('noise', None, 'tile')
The draws below stay inside these ranges and needn't reach their ends.
Inputs may be any that keep to these rules, and one draw needn't show every extreme that they name: The tiles fill a grid of 2 rows and 2 columns, each tile once, in an arrangement drawn per run; west and east neighbours run along a row, which closes into a loop; -1 stands for the missing north neighbour of the first row and south neighbour of the last row.
All inputs are finite; a program needn't handle non-finite values.
Results may differ from the reference program's by a relative error of at most 0.012.
Values may be sent and summed in bfloat16 or wider, within the bound.
A program may use at most 64 MiB of HBM per device.

```python
import math
import jax
import jax.numpy as jnp
from jax import lax

FIELDS = 69
WIDTH = 256
HEADS = 8
TILE = 16
FR_DEV = 4
LEVELS = 16
STEPS = 2
TILE_ROWS = 2
NTILES = 4
QUEUE = 32


def place_tile(placed, slot_index, tile_id):
    where_now = jnp.argmax((placed == tile_id).astype(jnp.int32)).astype(jnp.int32)
    held = placed[slot_index]
    placed = placed.at[where_now].set(held)
    return placed.at[slot_index].set(tile_id)


def draw_neighbours(key, part):
    column_count = NTILES // TILE_ROWS
    half_away = NTILES // 2
    order_key = jax.random.fold_in(key, 11)
    anchor_key = jax.random.fold_in(key, 12)
    column_key = jax.random.fold_in(key, 13)
    row_key = jax.random.fold_in(key, 14)
    placed = jax.random.permutation(order_key, NTILES).astype(jnp.int32)
    anchor = jax.random.randint(anchor_key, (), 0, NTILES).astype(jnp.int32)
    anchor_col = jax.random.randint(column_key, (), 0, column_count).astype(jnp.int32)
    anchor_row = jax.random.randint(row_key, (), 0, 2).astype(jnp.int32)
    other_row = (1 - anchor_row).astype(jnp.int32)
    first_slot = (anchor_row * column_count + anchor_col).astype(jnp.int32)
    east_slot = (anchor_row * column_count + (anchor_col + 1) % column_count).astype(jnp.int32)
    below_slot = (other_row * column_count + anchor_col).astype(jnp.int32)
    placed = place_tile(placed, first_slot, anchor)
    placed = place_tile(placed, east_slot, ((anchor + half_away) % NTILES).astype(jnp.int32))
    placed = place_tile(placed, below_slot, ((anchor + 1) % NTILES).astype(jnp.int32))
    where_is = jnp.argsort(placed, stable=True).astype(jnp.int32)
    row_of = where_is // column_count
    column_of = where_is % column_count
    west_tile = placed[row_of * column_count + (column_of + column_count - 1) % column_count]
    east_tile = placed[row_of * column_count + (column_of + 1) % column_count]
    north_tile = jnp.where(row_of > 0, placed[jnp.maximum(row_of - 1, 0) * column_count + column_of], -1)
    south_tile = jnp.where(row_of < TILE_ROWS - 1, placed[jnp.minimum(row_of + 1, TILE_ROWS - 1) * column_count + column_of], -1)
    return jnp.stack([west_tile, east_tile, north_tile, south_tile], axis=1).astype(jnp.int32)


def set_ends(entries, rng, smallest, high):
    longest = entries.shape.index(max(entries.shape))
    spots = []
    for shift in (0, 1):
        where = [jax.random.randint(jax.random.fold_in(rng, axis), (), 0, length) for axis, length in enumerate(entries.shape)]
        where[longest] = (where[longest] + shift) % entries.shape[longest]
        spots.append(tuple(where))
    return entries.at[spots[0]].set(smallest).at[spots[1]].set(high)


def block_scale(own_key, shape, cuts, smallest, top_value):
    loudness = 1.0
    for axis_at, shards_of in cuts:
        draws = jax.random.uniform(jax.random.fold_in(jax.random.fold_in(own_key, 6), axis_at), (shards_of,), jnp.float32, smallest / len(cuts), top_value / len(cuts))
        loudness = loudness * jnp.repeat(jnp.exp(draws), shape[axis_at] // shards_of).reshape((-1,) + (1,) * (len(shape) - 1 - axis_at))
    return loudness


def centred(stream_key, shape, deviation, most, pieces=(), kind=jnp.bfloat16):
    result = jax.random.normal(stream_key, shape, jnp.float32) * deviation
    if len(pieces) > 0:
        result = block_scale(stream_key, shape, pieces, -0.22, 0.18) * result
    return jnp.clip(result, min=-most, max=most).astype(kind)


def setup_inputs(seed: int = 0) -> dict:
    keys = jax.random.split(jax.random.key(seed), 14)
    queue_state = centred(keys[0], (QUEUE, FIELDS, NTILES, TILE * TILE), 1.0, 6.0, ((0, 8), (2, 4)), jnp.float32)
    fresh_noise = centred(keys[1], (STEPS, FIELDS, NTILES, TILE * TILE), 1.0, 6.0, ((2, 4),), jnp.float32)
    plan = jnp.clip(jnp.exp(jax.random.uniform(keys[2], (LEVELS + 1,), jnp.float32, math.log(0.5), math.log(2.0))), 0.5, 2.0)
    levels = set_ends(jax.random.randint(keys[3], (QUEUE,), 0, LEVELS), jax.random.fold_in(keys[3], 1), 0, LEVELS - 1).astype(jnp.int32)
    neighbours = draw_neighbours(jax.random.fold_in(keys[13], 71), 0)
    in_weight = centred(keys[5], (WIDTH, FIELDS), FIELDS ** -0.5, 0.75)
    level_embed = centred(keys[6], (WIDTH,), 0.5, 3.0, (), jnp.float32)
    conv_weight = centred(keys[7], (9, WIDTH, WIDTH), (9 * WIDTH) ** -0.5, 0.125)
    norm_gain = jnp.clip(1.0 + 0.1 * jax.random.normal(keys[8], (WIDTH,), jnp.float32), 0.5, 1.5)
    query_weight = centred(keys[9], (WIDTH, WIDTH), WIDTH ** -0.5, 0.375)
    memory_weight = centred(keys[10], (2 * WIDTH, WIDTH), WIDTH ** -0.5, 0.375)
    attend_out = centred(keys[11], (WIDTH, WIDTH), WIDTH ** -0.5, 0.375)
    decode_weight = centred(keys[12], (FIELDS, WIDTH), WIDTH ** -0.5, 0.375)
    return {"queue_state": queue_state, "fresh_noise": fresh_noise, "plan": plan, "levels": levels, "neighbours": neighbours, "in_weight": in_weight, "level_embed": level_embed, "conv_weight": conv_weight, "norm_gain": norm_gain, "query_weight": query_weight, "memory_weight": memory_weight, "attend_out": attend_out, "decode_weight": decode_weight}


def pick_tiles(source, tile_index):
    chosen = jnp.take(source, jnp.maximum(tile_index, 0), axis=1)
    return jnp.where((tile_index >= 0)[None, :, None], chosen, jnp.zeros_like(chosen))

def pad_tiles(frame_low, neighbours):
    west_col = pick_tiles(frame_low[:, :, :, TILE - 1], neighbours[:, 0])
    east_col = pick_tiles(frame_low[:, :, :, 0], neighbours[:, 1])
    middle = jnp.concatenate([west_col[..., None], frame_low, east_col[..., None]], axis=3)
    north_row = pick_tiles(middle[:, :, TILE - 1, :], neighbours[:, 2])
    south_row = pick_tiles(middle[:, :, 0, :], neighbours[:, 3])
    return jnp.concatenate([north_row[:, :, None, :], middle, south_row[:, :, None, :]], axis=2)

def frame_features(frame_state, sigma_one, in_weight, level_embed, conv_weight, norm_gain, neighbours):
    cell_count = NTILES * TILE * TILE
    in_scale = 1.0 / jnp.sqrt(sigma_one * sigma_one + 1.0)
    scaled = (in_scale * frame_state).reshape(FIELDS, cell_count).astype(jnp.bfloat16)
    lifted = jnp.dot(in_weight, scaled, preferred_element_type=jnp.float32) + jnp.log(sigma_one) * level_embed[:, None]
    lifted_low = lax.optimization_barrier(lifted.astype(jnp.bfloat16))
    padded = pad_tiles(lifted_low.reshape(WIDTH, NTILES, TILE, TILE), neighbours)
    convolved = jnp.zeros((WIDTH, cell_count), jnp.float32)
    for offset in range(9):
        down_by = offset // 3
        right_by = offset % 3
        window = padded[:, :, down_by:down_by + TILE, right_by:right_by + TILE].reshape(WIDTH, cell_count)
        convolved = convolved + jnp.dot(conv_weight[offset], window, preferred_element_type=jnp.float32)
    hidden = lax.optimization_barrier((lifted_low.astype(jnp.float32) + jax.nn.silu(convolved)).astype(jnp.bfloat16))
    widened = hidden.astype(jnp.float32)
    normed = (widened * lax.rsqrt(lax.optimization_barrier(jnp.mean(widened * widened, axis=0, keepdims=True)) + 1e-06) * norm_gain[:, None]).astype(jnp.bfloat16)
    return (hidden, normed)

def denoise(queue_now, sigmas, sigmas_next, neighbours, in_weight, level_embed, conv_weight, norm_gain, query_weight, memory_weight, attend_out, decode_weight):
    cell_count = NTILES * TILE * TILE
    head_size = WIDTH // HEADS

    def per_frame(frame_pair):
        frame_state, sigma_one = frame_pair
        hidden, normed = frame_features(frame_state, sigma_one, in_weight, level_embed, conv_weight, norm_gain, neighbours)
        queries = jnp.dot(query_weight, normed, preferred_element_type=jnp.float32).astype(jnp.bfloat16)
        memory = jnp.dot(memory_weight, normed, preferred_element_type=jnp.float32).astype(jnp.bfloat16)
        return (hidden, queries, memory)
    hidden_all, queries_all, memory_all = lax.map(per_frame, (queue_now, sigmas))
    memory_all = jnp.concatenate([memory_all, jnp.zeros((FR_DEV,) + memory_all.shape[1:], memory_all.dtype)], axis=0)

    def per_block(block_id):
        begin_at = (block_id * FR_DEV).astype(jnp.int32)
        block_query = lax.dynamic_slice_in_dim(queries_all, begin_at, FR_DEV, 0).astype(jnp.float32)
        block_query = block_query.reshape(FR_DEV, HEADS, head_size, cell_count)
        block_memory = lax.dynamic_slice_in_dim(memory_all, begin_at, 2 * FR_DEV, 0).astype(jnp.float32)
        key_heads = block_memory[:, :WIDTH].reshape(2 * FR_DEV, HEADS, head_size, cell_count)
        value_heads = block_memory[:, WIDTH:].reshape(2 * FR_DEV, HEADS, head_size, cell_count)
        scores = jnp.einsum('ihdm,jhdm->ijhm', block_query, key_heads, precision=lax.Precision.HIGHEST) * head_size ** (-0.5)
        usable = begin_at + jnp.arange(2 * FR_DEV, dtype=jnp.int32) < QUEUE
        scores = jnp.where(usable[None, :, None, None], scores, -jnp.inf)
        weights = lax.optimization_barrier(jax.nn.softmax(scores, axis=1).astype(jnp.bfloat16)).astype(jnp.float32)
        context = jnp.einsum('ijhm,jhdm->ihdm', weights, value_heads, precision=lax.Precision.HIGHEST)
        context = lax.optimization_barrier(context.astype(jnp.bfloat16)).astype(jnp.float32).reshape(FR_DEV, WIDTH, cell_count)
        attended = jnp.einsum('oc,icm->iom', attend_out.astype(jnp.float32), context, precision=lax.Precision.HIGHEST)
        block_hidden = lax.dynamic_slice_in_dim(hidden_all, begin_at, FR_DEV, 0).astype(jnp.float32)
        refined = lax.optimization_barrier((block_hidden + attended).astype(jnp.bfloat16)).astype(jnp.float32)
        projected = jnp.einsum('fc,icm->ifm', decode_weight.astype(jnp.float32), refined, precision=lax.Precision.HIGHEST)
        block_state = lax.dynamic_slice_in_dim(queue_now, begin_at, FR_DEV, 0).reshape(FR_DEV, FIELDS, cell_count)
        block_sigma = lax.dynamic_slice_in_dim(sigmas, begin_at, FR_DEV, 0)
        block_next = lax.dynamic_slice_in_dim(sigmas_next, begin_at, FR_DEV, 0)
        spread = block_sigma * block_sigma + 1.0
        denoised = (1.0 / spread)[:, None, None] * block_state + (block_sigma / jnp.sqrt(spread))[:, None, None] * projected
        return block_state + ((block_next - block_sigma) / block_sigma)[:, None, None] * (block_state - denoised)
    blocks = lax.map(per_block, jnp.arange(QUEUE // FR_DEV, dtype=jnp.int32))
    return blocks.reshape(queue_now.shape)

def reference(queue_state, fresh_noise, plan, levels, neighbours, in_weight, level_embed, conv_weight, norm_gain, query_weight, memory_weight, attend_out, decode_weight):
    sigmas = plan[levels]
    sigmas_next = plan[levels + 1]
    queue_now = queue_state
    for step_index in range(STEPS):
        entering = sigmas[QUEUE - 1] * fresh_noise[step_index]
        queue_now = jnp.concatenate([queue_now[1:], entering[None]], axis=0)
        queue_now = denoise(queue_now, sigmas, sigmas_next, neighbours, in_weight, level_embed, conv_weight, norm_gain, query_weight, memory_weight, attend_out, decode_weight)
    return queue_now
```

```python
import functools
import math

import jax
import jax.numpy as jnp
from jax import lax
from jax.experimental import pallas as pl
from jax.experimental.pallas import tpu as pltpu
from jax.sharding import PartitionSpec as P

HEADS = 8
MESH = pl.DeviceIdType.MESH
BF = jnp.bfloat16
F32 = jnp.float32


def dot_t(left, right):
    return lax.dot_general(left, right, (((1,), (1,)), ((), ())), preferred_element_type=F32)


def dot_n(left, right):
    return lax.dot_general(left, right, (((1,), (0,)), ((), ())), preferred_element_type=F32)


def kernel(
    groups, tiles, levels, plan, neighbours, queue, noise, in_weight, level_embed, conv_weight,
    norm_gain, query_weight, memory_weight, attend_out, decode_weight, out,
    frames_f32, own_low, next_low, second_low, own_edges, own_edges_1, next_edges, next_edges_1,
    second_edges, second_edges_1, noise_edges,
    sigma_own, sigma_next, lift_weight, head_sum, head_spread, pick, scaled, halo, halo_lifted,
    padded, hidden, normed, queries, memory, scores,
    send_sems, own_sems, next_sems, second_sems, noise_sems, frame_sems,
):
    frame_count, fields, cells = queue.shape
    steps = noise.shape[0]
    width = in_weight.shape[0]
    side = math.isqrt(cells)
    head_size = width // HEADS
    reach = 2 * frame_count
    own_edges = (own_edges, own_edges_1)
    next_edges = (next_edges, next_edges_1)
    second_edges = (second_edges, second_edges_1)
    me = lax.axis_index("tile")
    group = lax.axis_index("noise")
    is_last = group == groups - 1
    is_tail = group == groups - 2

    def tile_at(k):
        return lax.rem(me + k, tiles)

    barrier = pltpu.get_barrier_semaphore()
    for k in range(1, tiles):
        pl.semaphore_signal(
            barrier, 1, device_id={"noise": group, "tile": tile_at(k)}, device_id_type=MESH
        )
    for away in (-2, -1, 1, 2):
        @pl.when(jnp.logical_and(group + away >= 0, group + away < groups))
        def _():
            for k in range(tiles):
                pl.semaphore_signal(
                    barrier, 1, device_id={"noise": group + away, "tile": tile_at(k)},
                    device_id_type=MESH,
                )

    row = lax.broadcasted_iota(jnp.int32, (cells, 128), 0)
    lane = lax.broadcasted_iota(jnp.int32, (cells, 128), 1)
    part = lane % 64 // side
    spot = lane % side
    target = jnp.where(
        part == 0, spot, jnp.where(part == 1, (side - 1) * side + spot, jnp.where(
            part == 2, spot * side, spot * side + side - 1)))
    hit = row == target
    pick[0] = jnp.where(jnp.logical_and(hit, lane < 64), 1.0, 0.0).astype(BF)
    pick[1] = jnp.where(jnp.logical_and(hit, lane >= 64), 1.0, 0.0).astype(BF)
    channel = lax.broadcasted_iota(jnp.int32, (frame_count * width, 128), 0)
    head_lane = lax.broadcasted_iota(jnp.int32, (frame_count * width, 128), 1)
    head_sum[...] = jnp.where(channel // head_size == head_lane, 1.0, 0.0).astype(BF)
    channel = lax.broadcasted_iota(jnp.int32, (128, frame_count * width), 1)
    head_lane = lax.broadcasted_iota(jnp.int32, (128, frame_count * width), 0)
    head_spread[...] = jnp.where(channel // head_size == head_lane, 1.0, 0.0).astype(BF)
    lift_weight[...] = jnp.zeros_like(lift_weight)
    lift_weight[:, :fields] = in_weight[...]
    scaled[...] = jnp.zeros_like(scaled)
    halo[...] = jnp.zeros_like(halo)
    sigma_own[...] = jnp.ones_like(sigma_own)
    deltas = []
    for i in range(frame_count):
        sigma_own[i : i + 1] = jnp.full((1, 256), plan[levels[i]], F32)
        deltas.append(jnp.full((1, 256), plan[levels[i] + 1], F32))

    @pl.when(is_last)
    def _():
        sigma_next[...] = jnp.ones_like(sigma_next)
        next_low[...] = jnp.zeros_like(next_low)
        for edges in next_edges:
            edges[...] = jnp.zeros_like(edges)

    @pl.when(group >= groups - 2)
    def _():
        second_low[...] = jnp.zeros_like(second_low)
        for edges in second_edges:
            edges[...] = jnp.zeros_like(edges)

    frames_f32[:frame_count] = queue[...]
    for s in range(steps):
        both = dot_n(noise[s].astype(BF), pick[0] + pick[1])
        noise_edges[me, s] = both.astype(BF)

    west, east = neighbours[me, 0], neighbours[me, 1]
    north, south = neighbours[me, 2], neighbours[me, 3]
    north_in, south_in = jnp.maximum(north, 0), jnp.maximum(south, 0)
    north_west, north_east = neighbours[north_in, 0], neighbours[north_in, 1]
    south_west, south_east = neighbours[south_in, 0], neighbours[south_in, 1]
    around = [jnp.maximum(t, 0) for t in (south, north, east, west)]
    corner = [jnp.maximum(t, 0) for t in (south_east, south_west, north_east, north_west)]

    def copy(source, target_ref, send, recv, where):
        return pltpu.make_async_remote_copy(
            src_ref=source, dst_ref=target_ref, send_sem=send, recv_sem=recv,
            device_id=where, device_id_type=MESH,
        )

    def to_own(step, k, sender):
        return copy(
            own_edges[step].at[sender], own_edges[step].at[sender], send_sems.at[step, 0, k],
            own_sems.at[step, sender], {"noise": group, "tile": tile_at(k)},
        )

    def to_noise(k, sender):
        return copy(
            noise_edges.at[sender], noise_edges.at[sender], send_sems.at[0, 3, k],
            noise_sems.at[sender], {"noise": group, "tile": tile_at(k)},
        )

    def to_next(step, k, sender):
        return copy(
            own_edges[step].at[sender], next_edges[step].at[sender], send_sems.at[step, 1, k],
            next_sems.at[step, sender], {"noise": group - 1, "tile": tile_at(k)},
        )

    def to_second(step, k, sender):
        return copy(
            own_edges[step].at[sender, 0], second_edges[step].at[sender], send_sems.at[step, 2, k],
            second_sems.at[step, sender], {"noise": group - 2, "tile": tile_at(k)},
        )

    def frame_copy(step):
        return copy(
            own_low.at[step], next_low.at[step], send_sems.at[step, 4, 0], frame_sems.at[step, 0],
            {"noise": group - 1, "tile": me},
        )

    def front_copy(step):
        return copy(
            own_low.at[step, 0], second_low.at[step], send_sems.at[step, 4, 1],
            frame_sems.at[step, 1], {"noise": group - 2, "tile": me},
        )

    def sigma_copy():
        return copy(
            sigma_own, sigma_next, send_sems.at[0, 4, 2], frame_sems.at[0, 2],
            {"noise": group - 1, "tile": me},
        )

    def prepare(step):
        for f in range(frame_count):
            own_low[step, f] = frames_f32[f].astype(BF)
        for pair in range(frame_count // 2):
            edges = dot_n(own_low[step, 2 * pair], pick[0]) + dot_n(
                own_low[step, 2 * pair + 1], pick[1]
            )
            own_edges[step][me, pair] = edges.astype(BF)

    def send(step, first):
        for k in range(1, tiles):
            to_own(step, k, me).start()
            if first:
                to_noise(k, me).start()

        @pl.when(group >= 1)
        def _():
            if first:
                sigma_copy().start()
            frame_copy(step).start()
            for k in range(tiles):
                to_next(step, k, me).start()

        @pl.when(group >= 2)
        def _():
            front_copy(step).start()
            for k in range(tiles):
                to_second(step, k, me).start()

    def arrive(step, first):
        for k in range(1, tiles):
            to_own(step, k, tile_at(k)).wait_recv()
            if first:
                to_noise(k, tile_at(k)).wait_recv()

        @pl.when(group < groups - 1)
        def _():
            if first:
                sigma_copy().wait_recv()
            frame_copy(step).wait_recv()
            for k in range(tiles):
                to_next(step, k, tile_at(k)).wait_recv()

        @pl.when(group < groups - 2)
        def _():
            front_copy(step).wait_recv()
            for k in range(tiles):
                to_second(step, k, tile_at(k)).wait_recv()

    def sent(step, first):
        for k in range(1, tiles):
            to_own(step, k, me).wait_send()
            if first:
                to_noise(k, me).wait_send()

        @pl.when(group >= 1)
        def _():
            if first:
                sigma_copy().wait_send()
            frame_copy(step).wait_send()
            for k in range(tiles):
                to_next(step, k, me).wait_send()

        @pl.when(group >= 2)
        def _():
            front_copy(step).wait_send()
            for k in range(tiles):
                to_second(step, k, me).wait_send()

    def sigma_of(position):
        if position < frame_count:
            return sigma_own[position : position + 1]
        return sigma_next[position - frame_count : position - frame_count + 1]

    lane1 = lax.broadcasted_iota(jnp.int32, (1, 128), 1)
    slot = lane1 % 64 // side

    def halo_of(step, pair):
        if pair < frame_count // 2:
            load = lambda t: own_edges[step][t, pair].astype(F32)
        elif pair < frame_count:
            load = lambda t: next_edges[step][t, pair - frame_count // 2].astype(F32)
        else:
            load = lambda t: second_edges[step][t].astype(F32)
        fresh = None
        if pair == frame_count // 2:
            take, scale = jnp.logical_and(is_last, lane1 < 64), sigma_own
            fresh = True
        elif pair == frame_count:
            take, scale = jnp.logical_and(is_tail, lane1 < 64), sigma_next
            fresh = True

        def load_all(t):
            value = load(t)
            if fresh:
                fresh_value = noise_edges[t, step].astype(F32) * scale[
                    frame_count - 1 : frame_count, :128
                ]
                value = jnp.where(take, fresh_value, value)
            return value

        parts = [load_all(t) for t in around]
        middle = jnp.where(slot == 0, parts[0], jnp.where(
            slot == 1, parts[1], jnp.where(slot == 2, parts[2], parts[3])))
        parts = [load_all(t) for t in corner]
        place = lane1 % 64
        ends = jnp.where(place == 0, parts[0], jnp.where(
            place == side - 1, parts[1], jnp.where(place == side, parts[2], parts[3])))
        low = sigma_of(max(2 * pair - 1, 0))
        high = sigma_of(min(2 * pair, reach - 1))
        sigma = jnp.where(lane1 < 64, low[:, :128], high[:, :128])
        in_scale = lax.rsqrt(sigma * sigma + 1.0)
        halo[pair, :fields, :128] = middle * in_scale
        halo[pair, :fields, 128:] = ends * in_scale
        turned = halo[pair].T.astype(BF)
        rows = lax.broadcasted_iota(jnp.int32, (256, 1), 0) % 128
        bias = jnp.where(rows < 64, jnp.log(low), jnp.log(high)) * level_embed[...]
        lifted = dot_t(turned, lift_weight[...]) + bias
        kind = rows % 64 // side
        there = jnp.where(kind == 0, south, jnp.where(kind == 1, north, jnp.where(
            kind == 2, east, west)))
        lifted = jnp.where(there >= 0, lifted, 0.0)
        halo_lifted[pair] = lifted.astype(BF).astype(F32)

    def lift(step, position):
        sigma = sigma_of(position)
        in_scale = lax.rsqrt(sigma * sigma + 1.0)
        frame = position + 1
        if frame < frame_count:
            value = frames_f32[frame]
        elif frame < reach:
            value = next_low[step, frame - frame_count].astype(F32)
            if frame == frame_count:
                entering = sigma_own[frame_count - 1 : frame_count] * noise[step]
                value = jnp.where(is_last, entering, value)
                frames_f32[frame] = value
        else:
            value = second_low[step].astype(F32)
            entering = sigma_next[frame_count - 1 : frame_count] * noise[step]
            value = jnp.where(is_tail, entering, value)
        scaled[position % 2, :fields] = value * in_scale
        turned = scaled[position % 2].T.astype(BF)
        lifted = dot_t(turned, lift_weight[...]) + jnp.log(sigma) * level_embed[...]
        lifted = lifted.astype(BF).astype(F32)
        pair, base = frame // 2, frame % 2 * 64
        south_row = halo_lifted[pair, base : base + side]
        north_row = halo_lifted[pair, base + side : base + 2 * side]
        tall = jnp.concatenate([north_row, lifted, south_row], axis=0)
        padded[position, :, width : 2 * width] = tall.astype(BF)
        east_col, west_col = base + 2 * side, base + 3 * side
        ends = 128 + base
        west_rows = [ends + 2 * side - 1] + [west_col + y for y in range(side)] + [ends + side - 1]
        east_rows = [ends + side] + [east_col + y for y in range(side)] + [ends]

        def spread(rows):
            return jnp.concatenate([
                jnp.broadcast_to(halo_lifted[pair, r : r + 1], (side, width)) for r in rows
            ], axis=0)

        total = (side + 2) * side
        along = lax.broadcasted_iota(jnp.int32, (total, 1), 0) % side
        from_west = jnp.where(along == 0, spread(west_rows), pltpu.roll(tall, 1, 0))
        padded[position, :, :width] = from_west.astype(BF)
        from_east = jnp.where(along == side - 1, spread(east_rows), pltpu.roll(tall, total - 1, 0))
        padded[position, :, 2 * width :] = from_east.astype(BF)

    def convolve(index):
        total = None
        for offset in range(9):
            down, right = offset // 3, offset % 3
            window = padded[index, down * side : down * side + cells, right * width : (right + 1) * width]
            product = dot_t(window, conv_weight[offset])
            total = product if total is None else total + product
        centre = padded[index, side : side + cells, width : 2 * width].astype(F32)
        result = (centre + total / (1.0 + jnp.exp(-total))).astype(BF)
        hidden[index] = result
        widened = result.astype(F32)
        mean = jnp.mean(widened * widened, axis=1, keepdims=True)
        norm = (widened * lax.rsqrt(mean + 1e-06) * norm_gain[...]).astype(BF)
        memory[index] = dot_t(norm, memory_weight[...]).astype(BF)
        normed[index] = norm

    rows_at_once = 128

    def attend(chunk):
        begin = pl.multiple_of(chunk * rows_at_once, rows_at_once)
        here = pl.ds(begin, rows_at_once)
        most = None
        for j in range(reach):
            keys = memory[j, here, :width]
            products = jnp.concatenate([queries[i, here] * keys for i in range(frame_count)], axis=1)
            score = dot_n(products, head_sum[...]) * head_size ** (-0.5)
            if j >= frame_count:
                score = jnp.where(is_last, -jnp.inf, score)
            scores[j] = score
            most = score if most is None else jnp.maximum(most, score)
        total = None
        for j in range(reach):
            raised = jnp.exp(scores[j] - most)
            scores[j] = raised
            total = raised if total is None else total + raised
        inverse = 1.0 / total
        context = [None] * frame_count
        for j in range(reach):
            weight = (scores[j] * inverse).astype(BF)
            values = memory[j, here, width:].astype(F32)
            for i in range(frame_count):
                spread = dot_n(weight, head_spread[:, i * width : (i + 1) * width]) * values
                context[i] = spread if context[i] is None else context[i] + spread
        for i in range(frame_count):
            refined = hidden[i, here].astype(F32) + dot_t(context[i].astype(BF), attend_out[...])
            projected = dot_t(decode_weight[...], refined.astype(BF))
            sigma = sigma_own[i : i + 1, :rows_at_once]
            spread = sigma * sigma + 1.0
            frame = frames_f32[i + 1, :, here]
            denoised = (1.0 / spread) * frame + (sigma * lax.rsqrt(spread)) * projected
            change = (deltas[i][:, :rows_at_once] - sigma) / sigma
            frames_f32[i, :, here] = frame + change * (frame - denoised)

    for step in range(steps):
        prepare(step)
        if step == 0:
            reached = sum(
                jnp.where(jnp.logical_and(group + away >= 0, group + away < groups), tiles, 0)
                for away in (-2, -1, 1, 2)
            )
            pl.semaphore_wait(barrier, tiles - 1 + reached)
        send(step, step == 0)
        arrive(step, step == 0)
        for pair in range(frame_count + 1):
            halo_of(step, pair)
        for position in range(reach):
            lift(step, position)
        lax.fori_loop(0, reach, lambda index, c: (convolve(index), c)[1], 0)
        for i in range(frame_count):
            queries[i] = dot_t(normed[i], query_weight[...]).astype(BF)
        lax.fori_loop(0, cells // rows_at_once, lambda chunk, c: (attend(chunk), c)[1], 0)
        sent(step, step == 0)
    out[...] = frames_f32[:frame_count]


def shards(groups, tiles, queue_state, fresh_noise, plan, levels, neighbours, in_weight, level_embed,
           conv_weight, norm_gain, query_weight, memory_weight, attend_out, decode_weight):
    frames, fields, _, cells = queue_state.shape
    steps = fresh_noise.shape[0]
    width = in_weight.shape[0]
    side = math.isqrt(cells)
    reach = 2 * frames
    vmem = pl.BlockSpec(memory_space=pltpu.VMEM)
    smem = pl.BlockSpec(memory_space=pltpu.SMEM)
    dma = pltpu.SemaphoreType.DMA
    result = pl.pallas_call(
        functools.partial(kernel, groups, tiles),
        out_shape=jax.ShapeDtypeStruct((frames, fields, cells), F32),
        in_specs=[smem] * 3 + [vmem] * 10,
        out_specs=vmem,
        scratch_shapes=[
            pltpu.VMEM((frames + 1, fields, cells), F32),
            pltpu.VMEM((steps, frames, fields, cells), BF),
            pltpu.VMEM((steps, frames, fields, cells), BF),
            pltpu.VMEM((steps, fields, cells), BF),
            pltpu.VMEM((tiles, frames // 2, fields, 128), BF),
            pltpu.VMEM((tiles, frames // 2, fields, 128), BF),
            pltpu.VMEM((tiles, frames // 2, fields, 128), BF),
            pltpu.VMEM((tiles, frames // 2, fields, 128), BF),
            pltpu.VMEM((tiles, fields, 128), BF),
            pltpu.VMEM((tiles, fields, 128), BF),
            pltpu.VMEM((tiles, steps, fields, 128), BF),
            pltpu.VMEM((8, 256), F32),
            pltpu.VMEM((8, 256), F32),
            pltpu.VMEM((width, 128), BF),
            pltpu.VMEM((frames * width, 128), BF),
            pltpu.VMEM((128, frames * width), BF),
            pltpu.VMEM((2, cells, 128), BF),
            pltpu.VMEM((2, 128, cells), F32),
            pltpu.VMEM((frames + 1, 128, 256), F32),
            pltpu.VMEM((frames + 1, 256, width), F32),
            pltpu.VMEM((reach, (side + 2) * side, 3 * width), BF),
            pltpu.VMEM((reach, cells, width), BF),
            pltpu.VMEM((reach, cells, width), BF),
            pltpu.VMEM((frames, cells, width), BF),
            pltpu.VMEM((reach, cells, 2 * width), BF),
            pltpu.VMEM((reach, 128, 128), F32),
            dma((steps, 5, max(tiles, 3))),
            dma((steps, tiles)),
            dma((steps, tiles)),
            dma((steps, tiles)),
            dma((tiles,)),
            dma((steps, 3)),
        ],
        compiler_params=pltpu.CompilerParams(
            collective_id=0, has_side_effects=True, vmem_limit_bytes=56 * 1024 * 1024
        ),
    )(
        levels, plan, neighbours, queue_state.reshape(frames, fields, cells),
        fresh_noise.reshape(steps, fields, cells), in_weight, level_embed.reshape(1, width),
        conv_weight, norm_gain.reshape(1, width), query_weight, memory_weight, attend_out,
        decode_weight,
    )
    return result.reshape(queue_state.shape)


def solution(mesh):
    body = functools.partial(shards, mesh.shape["noise"], mesh.shape["tile"])
    in_specs = (
        P("noise", None, "tile", None), P(None, None, "tile", None), P(), P("noise"),
    ) + (P(),) * 9
    return jax.shard_map(
        body, mesh=mesh, in_specs=in_specs, out_specs=P("noise", None, "tile", None), check_vma=False
    )
```

```python
import functools
import math

import jax
import jax.numpy as jnp
from jax import lax
from jax.experimental import pallas as pl
from jax.experimental.pallas import tpu as pltpu
from jax.sharding import PartitionSpec as P

HEADS = 8
MESH = pl.DeviceIdType.MESH
BF = jnp.bfloat16
F32 = jnp.float32


def dot_t(left, right):
    return lax.dot_general(left, right, (((1,), (1,)), ((), ())), preferred_element_type=F32)


def dot_n(left, right):
    return lax.dot_general(left, right, (((1,), (0,)), ((), ())), preferred_element_type=F32)


def kernel(
    groups, tiles, levels, plan, neighbours, queue, noise_rows, in_weight, level_embed, conv_hbm,
    norm_gain, query_raw, memory_raw, attend_raw, decode_weight, out,
    conv_weight, query_weight, memory_weight, attend_out, noise, frames_f32, own_low, next_low, second_low, own_edges, own_edges_1, next_edges, next_edges_1,
    second_edges, second_edges_1, noise_edges,
    sigma_own, sigma_next, lift_weight, head_sum, head_spread, pick, scaled, halo, halo_lifted,
    padded, hidden, normed, queries, memory, load_sem,
    send_sems, own_sems, next_sems, second_sems, noise_sems, frame_sems,
):
    frame_count, fields, cells = padded.shape[0] // 2, in_weight.shape[0], hidden.shape[1]
    steps = own_low.shape[0]
    width = in_weight.shape[1]
    halves = cells // 128
    side = math.isqrt(cells)
    head_size = width // HEADS
    reach = 2 * frame_count
    own_edges = (own_edges, own_edges_1)
    next_edges = (next_edges, next_edges_1)
    second_edges = (second_edges, second_edges_1)
    me = lax.axis_index("tile")
    group = lax.axis_index("noise")
    is_last = group == groups - 1
    is_tail = group == groups - 2

    def tile_at(k):
        return lax.rem(me + k, tiles)

    load = pltpu.make_async_copy(conv_hbm, conv_weight, load_sem)
    load.start()
    barrier = pltpu.get_barrier_semaphore()
    for k in range(1, tiles):
        pl.semaphore_signal(
            barrier, 1, device_id={"noise": group, "tile": tile_at(k)}, device_id_type=MESH
        )
    for away in (-2, -1, 1, 2):
        @pl.when(jnp.logical_and(group + away >= 0, group + away < groups))
        def _():
            for k in range(tiles):
                pl.semaphore_signal(
                    barrier, 1, device_id={"noise": group + away, "tile": tile_at(k)},
                    device_id_type=MESH,
                )

    row = lax.broadcasted_iota(jnp.int32, (cells, 128), 0)
    lane = lax.broadcasted_iota(jnp.int32, (cells, 128), 1)
    part = lane % 64 // side
    spot = lane % side
    target = jnp.where(
        part == 0, spot, jnp.where(part == 1, (side - 1) * side + spot, jnp.where(
            part == 2, spot * side, spot * side + side - 1)))
    hit = row == target
    pick[0] = jnp.where(jnp.logical_and(hit, lane < 64), 1.0, 0.0).astype(BF)
    pick[1] = jnp.where(jnp.logical_and(hit, lane >= 64), 1.0, 0.0).astype(BF)
    pairs = frame_count * frame_count
    source = lax.broadcasted_iota(jnp.int32, (pairs // 2 * 128, 128), 0)
    target = lax.broadcasted_iota(jnp.int32, (pairs // 2 * 128, 128), 1)
    low = source % 128
    combo = source // 128 + jnp.where(low >= 64, pairs // 2, 0)
    head_sum[...] = jnp.where(target == combo * HEADS + low % HEADS, 1.0, 0.0).astype(BF)
    source = lax.broadcasted_iota(jnp.int32, (128, pairs * 128), 0)
    target = lax.broadcasted_iota(jnp.int32, (128, pairs * 128), 1)
    place = target // 128
    combo = place % frame_count * frame_count + place // frame_count
    head_spread[...] = jnp.where(source == combo * HEADS + target % HEADS, 1.0, 0.0).astype(BF)
    source = lax.broadcasted_iota(jnp.int32, (width, width), 1)
    target = lax.broadcasted_iota(jnp.int32, (width, width), 0)
    order = jnp.where(
        source == target % HEADS * head_size + target // HEADS, 1.0, 0.0
    ).astype(BF)
    lift_weight[...] = jnp.zeros_like(lift_weight)
    lift_weight[:fields] = in_weight[...]
    scaled[...] = jnp.zeros_like(scaled)
    halo[...] = jnp.zeros_like(halo)
    sigma_own[...] = jnp.ones_like(sigma_own)
    deltas = []
    for i in range(frame_count):
        sigma_own[i : i + 1] = jnp.full((1, 256), plan[levels[i]], F32)
        deltas.append(jnp.full((1, 256), plan[levels[i] + 1], F32))

    @pl.when(is_last)
    def _():
        sigma_next[...] = jnp.ones_like(sigma_next)
        next_low[...] = jnp.zeros_like(next_low)
        for edges in next_edges:
            edges[...] = jnp.zeros_like(edges)

    @pl.when(group >= groups - 2)
    def _():
        second_low[...] = jnp.zeros_like(second_low)
        for edges in second_edges:
            edges[...] = jnp.zeros_like(edges)

    for half in range(halves):
        across = slice(half * 128, (half + 1) * 128)
        for i in range(frame_count):
            frames_f32[i, :, across] = queue[pl.ds(i * halves * fields + half, fields, halves), :]
        for i in range(steps):
            noise[i, :, across] = noise_rows[pl.ds(i * halves * fields + half, fields, halves), :]
    for s in range(steps):
        both = dot_n(noise[s].astype(BF), pick[0] + pick[1])
        noise_edges[me, s] = both.astype(BF)

    west, east = neighbours[me, 0], neighbours[me, 1]
    north, south = neighbours[me, 2], neighbours[me, 3]
    north_in, south_in = jnp.maximum(north, 0), jnp.maximum(south, 0)
    north_west, north_east = neighbours[north_in, 0], neighbours[north_in, 1]
    south_west, south_east = neighbours[south_in, 0], neighbours[south_in, 1]
    around = [jnp.maximum(t, 0) for t in (south, north, east, west)]
    corner = [jnp.maximum(t, 0) for t in (south_east, south_west, north_east, north_west)]

    def copy(source, target_ref, send, recv, where):
        return pltpu.make_async_remote_copy(
            src_ref=source, dst_ref=target_ref, send_sem=send, recv_sem=recv,
            device_id=where, device_id_type=MESH,
        )

    def to_own(step, k, sender):
        return copy(
            own_edges[step].at[sender], own_edges[step].at[sender], send_sems.at[step, 0, k],
            own_sems.at[step, sender], {"noise": group, "tile": tile_at(k)},
        )

    def to_noise(k, sender):
        return copy(
            noise_edges.at[sender], noise_edges.at[sender], send_sems.at[0, 3, k],
            noise_sems.at[sender], {"noise": group, "tile": tile_at(k)},
        )

    def to_next(step, k, sender):
        return copy(
            own_edges[step].at[sender], next_edges[step].at[sender], send_sems.at[step, 1, k],
            next_sems.at[step, sender], {"noise": group - 1, "tile": tile_at(k)},
        )

    def to_second(step, k, sender):
        return copy(
            own_edges[step].at[sender, 0], second_edges[step].at[sender], send_sems.at[step, 2, k],
            second_sems.at[step, sender], {"noise": group - 2, "tile": tile_at(k)},
        )

    def frame_copy(step):
        return copy(
            own_low.at[step], next_low.at[step], send_sems.at[step, 4, 0], frame_sems.at[step, 0],
            {"noise": group - 1, "tile": me},
        )

    def front_copy(step):
        return copy(
            own_low.at[step, 0], second_low.at[step], send_sems.at[step, 4, 1],
            frame_sems.at[step, 1], {"noise": group - 2, "tile": me},
        )

    def sigma_copy():
        return copy(
            sigma_own, sigma_next, send_sems.at[0, 4, 2], frame_sems.at[0, 2],
            {"noise": group - 1, "tile": me},
        )

    def prepare(step):
        for f in range(frame_count):
            own_low[step, f] = frames_f32[f].astype(BF)
        for pair in range(frame_count // 2):
            edges = dot_n(own_low[step, 2 * pair], pick[0]) + dot_n(
                own_low[step, 2 * pair + 1], pick[1]
            )
            own_edges[step][me, pair] = edges.astype(BF)

    def send(step, first):
        for k in range(1, tiles):
            to_own(step, k, me).start()
            if first:
                to_noise(k, me).start()

        @pl.when(group >= 1)
        def _():
            if first:
                sigma_copy().start()
            frame_copy(step).start()
            for k in range(1, tiles):
                to_next(step, k, me).start()

        @pl.when(group >= 2)
        def _():
            front_copy(step).start()
            for k in range(1, tiles):
                to_second(step, k, me).start()

    def arrive_own(step, first):
        for k in range(1, tiles):
            to_own(step, k, tile_at(k)).wait_recv()
            if first:
                to_noise(k, tile_at(k)).wait_recv()

    def arrive_next(step, first):
        @pl.when(group < groups - 1)
        def _():
            if first:
                sigma_copy().wait_recv()
            frame_copy(step).wait_recv()
            for k in range(1, tiles):
                to_next(step, k, tile_at(k)).wait_recv()

    def arrive_second(step):
        @pl.when(group < groups - 2)
        def _():
            front_copy(step).wait_recv()
            for k in range(1, tiles):
                to_second(step, k, tile_at(k)).wait_recv()

    def sent(step, first):
        for k in range(1, tiles):
            to_own(step, k, me).wait_send()
            if first:
                to_noise(k, me).wait_send()

        @pl.when(group >= 1)
        def _():
            if first:
                sigma_copy().wait_send()
            frame_copy(step).wait_send()
            for k in range(1, tiles):
                to_next(step, k, me).wait_send()

        @pl.when(group >= 2)
        def _():
            front_copy(step).wait_send()
            for k in range(1, tiles):
                to_second(step, k, me).wait_send()

    def sigma_of(position):
        if position < frame_count:
            return sigma_own[position : position + 1]
        return sigma_next[position - frame_count : position - frame_count + 1]

    lane1 = lax.broadcasted_iota(jnp.int32, (1, 128), 1)
    slot = lane1 % 64 // side

    def halo_of(step, pair):
        if pair < frame_count // 2:
            load = lambda t: own_edges[step][t, pair].astype(F32)
        elif pair < frame_count:
            load = lambda t: next_edges[step][t, pair - frame_count // 2].astype(F32)
        else:
            load = lambda t: second_edges[step][t].astype(F32)
        fresh = None
        if pair == frame_count // 2:
            take, scale = jnp.logical_and(is_last, lane1 < 64), sigma_own
            fresh = True
        elif pair == frame_count:
            take, scale = jnp.logical_and(is_tail, lane1 < 64), sigma_next
            fresh = True

        def load_all(t):
            value = load(t)
            if fresh:
                fresh_value = noise_edges[t, step].astype(F32) * scale[
                    frame_count - 1 : frame_count, :128
                ]
                value = jnp.where(take, fresh_value, value)
            return value

        parts = [load_all(t) for t in around]
        middle = jnp.where(slot == 0, parts[0], jnp.where(
            slot == 1, parts[1], jnp.where(slot == 2, parts[2], parts[3])))
        parts = [load_all(t) for t in corner]
        place = lane1 % 64
        ends = jnp.where(place == 0, parts[0], jnp.where(
            place == side - 1, parts[1], jnp.where(place == side, parts[2], parts[3])))
        low = sigma_of(max(2 * pair - 1, 0))
        high = sigma_of(min(2 * pair, reach - 1))
        sigma = jnp.where(lane1 < 64, low[:, :128], high[:, :128])
        in_scale = lax.rsqrt(sigma * sigma + 1.0)
        halo[pair, :fields, :128] = middle * in_scale
        halo[pair, :fields, 128:] = ends * in_scale
        turned = halo[pair].T.astype(BF)
        rows = lax.broadcasted_iota(jnp.int32, (256, 1), 0) % 128
        bias = jnp.where(rows < 64, jnp.log(low), jnp.log(high)) * level_embed[...]
        lifted = dot_n(turned, lift_weight[...]) + bias
        kind = rows % 64 // side
        there = jnp.where(kind == 0, south, jnp.where(kind == 1, north, jnp.where(
            kind == 2, east, west)))
        lifted = jnp.where(there >= 0, lifted, 0.0)
        halo_lifted[pair] = lifted.astype(BF).astype(F32)

    def lift(step, position):
        sigma = sigma_of(position)
        in_scale = lax.rsqrt(sigma * sigma + 1.0)
        frame = position + 1
        if frame < frame_count:
            value = frames_f32[frame]
        elif frame < reach:
            value = next_low[step, frame - frame_count].astype(F32)
            if frame == frame_count:
                entering = sigma_own[frame_count - 1 : frame_count] * noise[step]
                value = jnp.where(is_last, entering, value)
                frames_f32[frame] = value
        else:
            value = second_low[step].astype(F32)
            entering = sigma_next[frame_count - 1 : frame_count] * noise[step]
            value = jnp.where(is_tail, entering, value)
        scaled[position % 2, :fields] = value * in_scale
        turned = scaled[position % 2].T.astype(BF)
        lifted = dot_n(turned, lift_weight[...]) + jnp.log(sigma) * level_embed[...]
        lifted = lifted.astype(BF).astype(F32)
        pair, base = frame // 2, frame % 2 * 64
        south_row = halo_lifted[pair, base : base + side]
        north_row = halo_lifted[pair, base + side : base + 2 * side]
        tall = jnp.concatenate([north_row, lifted, south_row], axis=0)
        padded[position, :, width : 2 * width] = tall.astype(BF)
        east_col, west_col = base + 2 * side, base + 3 * side
        ends = 128 + base
        west_rows = [ends + 2 * side - 1] + [west_col + y for y in range(side)] + [ends + side - 1]
        east_rows = [ends + side] + [east_col + y for y in range(side)] + [ends]

        def spread(rows):
            return jnp.concatenate([
                jnp.broadcast_to(halo_lifted[pair, r : r + 1], (side, width)) for r in rows
            ], axis=0)

        total = (side + 2) * side
        along = lax.broadcasted_iota(jnp.int32, (total, 1), 0) % side
        from_west = jnp.where(along == 0, spread(west_rows), pltpu.roll(tall, 1, 0))
        padded[position, :, :width] = from_west.astype(BF)
        from_east = jnp.where(along == side - 1, spread(east_rows), pltpu.roll(tall, total - 1, 0))
        padded[position, :, 2 * width :] = from_east.astype(BF)

    def convolve(index):
        total = None
        for offset in range(9):
            down, right = offset // 3, offset % 3
            window = padded[index, down * side : down * side + cells, right * width : (right + 1) * width]
            product = dot_t(window, conv_weight[offset])
            total = product if total is None else total + product
        centre = padded[index, side : side + cells, width : 2 * width].astype(F32)
        result = (centre + total / (1.0 + jnp.exp(-total))).astype(BF)
        hidden[index] = result
        widened = result.astype(F32)
        mean = jnp.mean(widened * widened, axis=1, keepdims=True)
        norm = (widened * lax.rsqrt(mean + 1e-06) * norm_gain[...]).astype(BF)
        memory[index] = dot_t(norm, memory_weight[...]).astype(BF)
        normed[index] = norm

    rows_at_once = 128

    def attend(chunk):
        begin = pl.multiple_of(chunk * rows_at_once, rows_at_once)
        here = pl.ds(begin, rows_at_once)
        lower = lax.broadcasted_iota(jnp.int32, (1, 128), 1) < 64
        asked = [queries[i, here].astype(F32) for i in range(frame_count)]

        def partial(i, j):
            product = asked[i] * memory[j, here, :width].astype(F32)
            total = product[:, :128]
            for start in range(128, width, 128):
                total = total + product[:, start : start + 128]
            return total

        def score_block(first):
            pieces = []
            for c in range(pairs // 2):
                later = c + pairs // 2
                one = partial(c % frame_count, first + c // frame_count)
                two = partial(later % frame_count, first + later // frame_count)
                swapped = pltpu.roll(jnp.where(lower, two, one), 64, 1)
                pieces.append((jnp.where(lower, one, two) + swapped).astype(BF))
            return dot_n(jnp.concatenate(pieces, axis=1), head_sum[...]) * head_size ** (-0.5)

        near = score_block(0)
        far = jnp.where(is_last, -jnp.inf, score_block(frame_count))
        most = jnp.maximum(near, far)
        most = jnp.maximum(most, pltpu.roll(most, 64, 1))
        most = jnp.maximum(most, pltpu.roll(most, 32, 1))
        near = jnp.exp(near - most)
        far = jnp.exp(far - most)
        total = near + far
        total = total + pltpu.roll(total, 64, 1)
        total = total + pltpu.roll(total, 32, 1)
        inverse = 1.0 / total
        near = (near * inverse).astype(BF)
        far = (far * inverse).astype(BF)
        for i in range(frame_count):
            context = None
            columns = slice(i * frame_count * 128, (i + 1) * frame_count * 128)
            for block, weight in enumerate((near, far)):
                spread = dot_n(weight, head_spread[:, columns])
                for at in range(frame_count):
                    wide = spread[:, at * 128 : (at + 1) * 128]
                    values = memory[block * frame_count + at, here, width:].astype(F32)
                    term = jnp.concatenate([wide] * (width // 128), axis=1) * values
                    context = term if context is None else context + term
            refined = hidden[i, here].astype(F32) + dot_t(context.astype(BF), attend_out[...])
            projected = dot_t(decode_weight[...], refined.astype(BF))
            sigma = sigma_own[i : i + 1, :rows_at_once]
            spread = sigma * sigma + 1.0
            frame = frames_f32[i + 1, :, here]
            denoised = (1.0 / spread) * frame + (sigma * lax.rsqrt(spread)) * projected
            change = (deltas[i][:, :rows_at_once] - sigma) / sigma
            frames_f32[i, :, here] = frame + change * (frame - denoised)

    for step in range(steps):
        prepare(step)
        if step == 0:
            reached = sum(
                jnp.where(jnp.logical_and(group + away >= 0, group + away < groups), tiles, 0)
                for away in (-2, -1, 1, 2)
            )
            pl.semaphore_wait(barrier, tiles - 1 + reached)
        send(step, step == 0)
        if step == 0:
            query_weight[...] = dot_n(order, query_raw[...]).astype(BF)
            memory_weight[:width] = dot_n(order, memory_raw[:width]).astype(BF)
            memory_weight[width:] = dot_n(order, memory_raw[width:]).astype(BF)
            attend_out[...] = dot_t(attend_raw[...], order).astype(BF)
        half = frame_count // 2
        arrive_own(step, step == 0)
        for pair in range(half):
            halo_of(step, pair)
        for position in range(frame_count - 1):
            lift(step, position)
        if step == 0:
            load.wait()
        lax.fori_loop(0, frame_count - 1, lambda index, c: (convolve(index), c)[1], 0)
        arrive_next(step, step == 0)
        for pair in range(half, frame_count):
            halo_of(step, pair)
        for position in range(frame_count - 1, reach - 1):
            lift(step, position)
        arrive_second(step)
        halo_of(step, frame_count)
        lift(step, reach - 1)
        lax.fori_loop(frame_count - 1, reach, lambda index, c: (convolve(index), c)[1], 0)
        for i in range(frame_count):
            queries[i] = dot_t(normed[i], query_weight[...]).astype(BF)
        lax.fori_loop(0, cells // rows_at_once, lambda chunk, c: (attend(chunk), c)[1], 0)
        sent(step, step == 0)
    for half in range(halves):
        across = slice(half * 128, (half + 1) * 128)
        for i in range(frame_count):
            out[pl.ds(i * halves * fields + half, fields, halves), :] = frames_f32[i, :, across]


def shards(groups, tiles, queue_state, fresh_noise, plan, levels, neighbours, in_weight, level_embed,
           conv_weight, norm_gain, query_weight, memory_weight, attend_out, decode_weight):
    frames, fields, _, cells = queue_state.shape
    steps = fresh_noise.shape[0]
    width = in_weight.shape[0]
    side = math.isqrt(cells)
    reach = 2 * frames
    vmem = pl.BlockSpec(memory_space=pltpu.VMEM)
    smem = pl.BlockSpec(memory_space=pltpu.SMEM)
    dma = pltpu.SemaphoreType.DMA
    result = pl.pallas_call(
        functools.partial(kernel, groups, tiles),
        out_shape=jax.ShapeDtypeStruct((frames * fields * cells // 128, 128), F32),
        in_specs=[smem] * 3 + [vmem] * 4 + [pl.BlockSpec(memory_space=pl.ANY)] + [vmem] * 5,
        out_specs=vmem,
        scratch_shapes=[
            pltpu.VMEM(conv_weight.shape, BF),
            pltpu.VMEM(query_weight.shape, BF),
            pltpu.VMEM(memory_weight.shape, BF),
            pltpu.VMEM(attend_out.shape, BF),
            pltpu.VMEM((steps, fields, cells), F32),
            pltpu.VMEM((frames + 1, fields, cells), F32),
            pltpu.VMEM((steps, frames, fields, cells), BF),
            pltpu.VMEM((steps, frames, fields, cells), BF),
            pltpu.VMEM((steps, fields, cells), BF),
            pltpu.VMEM((tiles, frames // 2, fields, 128), BF),
            pltpu.VMEM((tiles, frames // 2, fields, 128), BF),
            pltpu.VMEM((tiles, frames // 2, fields, 128), BF),
            pltpu.VMEM((tiles, frames // 2, fields, 128), BF),
            pltpu.VMEM((tiles, fields, 128), BF),
            pltpu.VMEM((tiles, fields, 128), BF),
            pltpu.VMEM((tiles, steps, fields, 128), BF),
            pltpu.VMEM((8, 256), F32),
            pltpu.VMEM((8, 256), F32),
            pltpu.VMEM((128, width), BF),
            pltpu.VMEM((frames * frames * 64, 128), BF),
            pltpu.VMEM((128, frames * frames * 128), BF),
            pltpu.VMEM((2, cells, 128), BF),
            pltpu.VMEM((2, 128, cells), F32),
            pltpu.VMEM((frames + 1, 128, 256), F32),
            pltpu.VMEM((frames + 1, 256, width), F32),
            pltpu.VMEM((reach, (side + 2) * side, 3 * width), BF),
            pltpu.VMEM((reach, cells, width), BF),
            pltpu.VMEM((reach, cells, width), BF),
            pltpu.VMEM((frames, cells, width), BF),
            pltpu.VMEM((reach, cells, 2 * width), BF),
            dma,
            dma((steps, 5, max(tiles, 3))),
            dma((steps, tiles)),
            dma((steps, tiles)),
            dma((steps, tiles)),
            dma((tiles,)),
            dma((steps, 3)),
        ],
        compiler_params=pltpu.CompilerParams(
            collective_id=0, has_side_effects=True, vmem_limit_bytes=56 * 1024 * 1024
        ),
    )(
        levels, plan, neighbours, queue_state.reshape(-1, 128),
        fresh_noise.reshape(-1, 128), in_weight.T, level_embed.reshape(1, width),
        conv_weight, norm_gain.reshape(1, width), query_weight, memory_weight, attend_out,
        decode_weight,
    )
    return result.reshape(queue_state.shape)


def solution(mesh):
    body = functools.partial(shards, mesh.shape["noise"], mesh.shape["tile"])
    in_specs = (
        P("noise", None, "tile", None), P(None, None, "tile", None), P(), P("noise"),
    ) + (P(),) * 9
    return jax.shard_map(
        body, mesh=mesh, in_specs=in_specs, out_specs=P("noise", None, "tile", None), check_vma=False
    )
```

```python
import functools
import math

import jax
import jax.numpy as jnp
from jax import lax
from jax.experimental import pallas as pl
from jax.experimental.pallas import tpu as pltpu
from jax.sharding import PartitionSpec as P

HEADS = 8
MESH = pl.DeviceIdType.MESH
BF = jnp.bfloat16
F32 = jnp.float32


def dot_t(left, right):
    return lax.dot_general(left, right, (((1,), (1,)), ((), ())), preferred_element_type=F32)


def dot_n(left, right):
    return lax.dot_general(left, right, (((1,), (0,)), ((), ())), preferred_element_type=F32)


def kernel(
    groups, tiles, levels, plan, neighbours, queue, noise_rows, in_weight, level_embed, conv_hbm,
    norm_gain, query_raw, memory_raw, attend_raw, decode_weight, out,
    conv_weight, query_weight, memory_weight, attend_out, noise, frames_f32, own_low, next_low, second_low, own_edges, own_edges_1, next_edges, next_edges_1,
    second_edges, second_edges_1, noise_edges,
    sigma_own, sigma_next, lift_weight, head_sum, head_spread, pick, scaled, halo, halo_lifted,
    padded, hidden, normed, queries, memory, load_sem,
    send_sems, own_sems, next_sems, second_sems, noise_sems, frame_sems,
):
    frame_count, fields, cells = padded.shape[0] // 2, in_weight.shape[0], hidden.shape[1]
    steps = own_low.shape[0]
    width = in_weight.shape[1]
    halves = cells // 128
    side = math.isqrt(cells)
    head_size = width // HEADS
    reach = 2 * frame_count
    own_edges = (own_edges, own_edges_1)
    next_edges = (next_edges, next_edges_1)
    second_edges = (second_edges, second_edges_1)
    me = lax.axis_index("tile")
    group = lax.axis_index("noise")
    is_last = group == groups - 1
    is_tail = group == groups - 2

    def tile_at(k):
        return lax.rem(me + k, tiles)

    load = pltpu.make_async_copy(conv_hbm, conv_weight, load_sem)
    load.start()
    barrier = pltpu.get_barrier_semaphore()
    for k in range(1, tiles):
        pl.semaphore_signal(
            barrier, 1, device_id={"noise": group, "tile": tile_at(k)}, device_id_type=MESH
        )
    for away in (-2, -1, 1, 2):
        @pl.when(jnp.logical_and(group + away >= 0, group + away < groups))
        def _():
            for k in range(tiles):
                pl.semaphore_signal(
                    barrier, 1, device_id={"noise": group + away, "tile": tile_at(k)},
                    device_id_type=MESH,
                )

    row = lax.broadcasted_iota(jnp.int32, (cells, 128), 0)
    lane = lax.broadcasted_iota(jnp.int32, (cells, 128), 1)
    part = lane % 64 // side
    spot = lane % side
    target = jnp.where(
        part == 0, spot, jnp.where(part == 1, (side - 1) * side + spot, jnp.where(
            part == 2, spot * side, spot * side + side - 1)))
    hit = row == target
    pick[0] = jnp.where(jnp.logical_and(hit, lane < 64), 1.0, 0.0).astype(BF)
    pick[1] = jnp.where(jnp.logical_and(hit, lane >= 64), 1.0, 0.0).astype(BF)
    pairs = frame_count * frame_count
    source = lax.broadcasted_iota(jnp.int32, (pairs * 128, 128), 0)
    target = lax.broadcasted_iota(jnp.int32, (pairs * 128, 128), 1)
    low = source % 128
    combo = source // 128
    head_sum[...] = jnp.where(target == combo * HEADS + low % HEADS, 1.0, 0.0).astype(BF)
    source = lax.broadcasted_iota(jnp.int32, (128, pairs * 128), 0)
    target = lax.broadcasted_iota(jnp.int32, (128, pairs * 128), 1)
    place = target // 128
    combo = place % frame_count * frame_count + place // frame_count
    head_spread[...] = jnp.where(source == combo * HEADS + target % HEADS, 1.0, 0.0).astype(BF)
    source = lax.broadcasted_iota(jnp.int32, (width, width), 1)
    target = lax.broadcasted_iota(jnp.int32, (width, width), 0)
    order = jnp.where(
        source == target % HEADS * head_size + target // HEADS, 1.0, 0.0
    ).astype(BF)
    lift_weight[...] = jnp.zeros_like(lift_weight)
    lift_weight[:fields] = in_weight[...]
    scaled[...] = jnp.zeros_like(scaled)
    halo[...] = jnp.zeros_like(halo)
    sigma_own[...] = jnp.ones_like(sigma_own)
    deltas = []
    for i in range(frame_count):
        sigma_own[i : i + 1] = jnp.full((1, 256), plan[levels[i]], F32)
        deltas.append(jnp.full((1, 256), plan[levels[i] + 1], F32))

    @pl.when(is_last)
    def _():
        sigma_next[...] = jnp.ones_like(sigma_next)
        next_low[...] = jnp.zeros_like(next_low)
        for edges in next_edges:
            edges[...] = jnp.zeros_like(edges)

    @pl.when(group >= groups - 2)
    def _():
        second_low[...] = jnp.zeros_like(second_low)
        for edges in second_edges:
            edges[...] = jnp.zeros_like(edges)

    for half in range(halves):
        across = slice(half * 128, (half + 1) * 128)
        for i in range(frame_count):
            frames_f32[i, :, across] = queue[pl.ds(i * halves * fields + half, fields, halves), :]
        for i in range(steps):
            noise[i, :, across] = noise_rows[i, :, 0, across]
    for s in range(steps):
        both = dot_n(noise[s].astype(BF), pick[0] + pick[1])
        noise_edges[me, s] = both.astype(BF)

    west, east = neighbours[me, 0], neighbours[me, 1]
    north, south = neighbours[me, 2], neighbours[me, 3]
    north_in, south_in = jnp.maximum(north, 0), jnp.maximum(south, 0)
    north_west, north_east = neighbours[north_in, 0], neighbours[north_in, 1]
    south_west, south_east = neighbours[south_in, 0], neighbours[south_in, 1]
    around = [jnp.maximum(t, 0) for t in (south, north, east, west)]
    corner = [jnp.maximum(t, 0) for t in (south_east, south_west, north_east, north_west)]

    def copy(source, target_ref, send, recv, where):
        return pltpu.make_async_remote_copy(
            src_ref=source, dst_ref=target_ref, send_sem=send, recv_sem=recv,
            device_id=where, device_id_type=MESH,
        )

    def to_own(step, k, sender):
        return copy(
            own_edges[step].at[sender], own_edges[step].at[sender], send_sems.at[step, 0, k],
            own_sems.at[step, sender], {"noise": group, "tile": tile_at(k)},
        )

    def to_noise(k, sender):
        return copy(
            noise_edges.at[sender], noise_edges.at[sender], send_sems.at[0, 3, k],
            noise_sems.at[sender], {"noise": group, "tile": tile_at(k)},
        )

    def to_next(step, k, sender):
        return copy(
            own_edges[step].at[sender], next_edges[step].at[sender], send_sems.at[step, 1, k],
            next_sems.at[step, sender], {"noise": group - 1, "tile": tile_at(k)},
        )

    def to_second(step, k, sender):
        return copy(
            own_edges[step].at[sender, 0], second_edges[step].at[sender], send_sems.at[step, 2, k],
            second_sems.at[step, sender], {"noise": group - 2, "tile": tile_at(k)},
        )

    def frame_copy(step):
        return copy(
            own_low.at[step], next_low.at[step], send_sems.at[step, 4, 0], frame_sems.at[step, 0],
            {"noise": group - 1, "tile": me},
        )

    def front_copy(step):
        return copy(
            own_low.at[step, 0], second_low.at[step], send_sems.at[step, 4, 1],
            frame_sems.at[step, 1], {"noise": group - 2, "tile": me},
        )

    def sigma_copy():
        return copy(
            sigma_own, sigma_next, send_sems.at[0, 4, 2], frame_sems.at[0, 2],
            {"noise": group - 1, "tile": me},
        )

    def prepare(step):
        for f in range(frame_count):
            own_low[step, f] = frames_f32[f].astype(BF)
        for pair in range(frame_count // 2):
            edges = dot_n(own_low[step, 2 * pair], pick[0]) + dot_n(
                own_low[step, 2 * pair + 1], pick[1]
            )
            own_edges[step][me, pair] = edges.astype(BF)

    def send(step, first):
        for k in range(1, tiles):
            to_own(step, k, me).start()
            if first:
                to_noise(k, me).start()

        @pl.when(group >= 1)
        def _():
            if first:
                sigma_copy().start()
            frame_copy(step).start()
            for k in range(1, tiles):
                to_next(step, k, me).start()

        @pl.when(group >= 2)
        def _():
            front_copy(step).start()
            for k in range(1, tiles):
                to_second(step, k, me).start()

    def arrive_own(step, first):
        for k in range(1, tiles):
            to_own(step, k, tile_at(k)).wait_recv()
            if first:
                to_noise(k, tile_at(k)).wait_recv()

    def arrive_next(step, first):
        @pl.when(group < groups - 1)
        def _():
            if first:
                sigma_copy().wait_recv()
            frame_copy(step).wait_recv()
            for k in range(1, tiles):
                to_next(step, k, tile_at(k)).wait_recv()

    def arrive_second(step):
        @pl.when(group < groups - 2)
        def _():
            front_copy(step).wait_recv()
            for k in range(1, tiles):
                to_second(step, k, tile_at(k)).wait_recv()

    def sent(step, first):
        for k in range(1, tiles):
            to_own(step, k, me).wait_send()
            if first:
                to_noise(k, me).wait_send()

        @pl.when(group >= 1)
        def _():
            if first:
                sigma_copy().wait_send()
            frame_copy(step).wait_send()
            for k in range(1, tiles):
                to_next(step, k, me).wait_send()

        @pl.when(group >= 2)
        def _():
            front_copy(step).wait_send()
            for k in range(1, tiles):
                to_second(step, k, me).wait_send()

    def sigma_of(position):
        if position < frame_count:
            return sigma_own[position : position + 1]
        return sigma_next[position - frame_count : position - frame_count + 1]

    lane1 = lax.broadcasted_iota(jnp.int32, (1, 128), 1)
    slot = lane1 % 64 // side

    def halo_of(step, pair):
        if pair < frame_count // 2:
            load = lambda t: own_edges[step][t, pair].astype(F32)
        elif pair < frame_count:
            load = lambda t: next_edges[step][t, pair - frame_count // 2].astype(F32)
        else:
            load = lambda t: second_edges[step][t].astype(F32)
        fresh = None
        if pair == frame_count // 2:
            take, scale = jnp.logical_and(is_last, lane1 < 64), sigma_own
            fresh = True
        elif pair == frame_count:
            take, scale = jnp.logical_and(is_tail, lane1 < 64), sigma_next
            fresh = True

        def load_all(t):
            value = load(t)
            if fresh:
                fresh_value = noise_edges[t, step].astype(F32) * scale[
                    frame_count - 1 : frame_count, :128
                ]
                value = jnp.where(take, fresh_value, value)
            return value

        parts = [load_all(t) for t in around]
        middle = jnp.where(slot == 0, parts[0], jnp.where(
            slot == 1, parts[1], jnp.where(slot == 2, parts[2], parts[3])))
        parts = [load_all(t) for t in corner]
        place = lane1 % 64
        ends = jnp.where(place == 0, parts[0], jnp.where(
            place == side - 1, parts[1], jnp.where(place == side, parts[2], parts[3])))
        low = sigma_of(max(2 * pair - 1, 0))
        high = sigma_of(min(2 * pair, reach - 1))
        sigma = jnp.where(lane1 < 64, low[:, :128], high[:, :128])
        in_scale = lax.rsqrt(sigma * sigma + 1.0)
        halo[pair, :fields, :128] = middle * in_scale
        halo[pair, :fields, 128:] = ends * in_scale
        turned = halo[pair].T.astype(BF)
        rows = lax.broadcasted_iota(jnp.int32, (256, 1), 0) % 128
        bias = jnp.where(rows < 64, jnp.log(low), jnp.log(high)) * level_embed[...]
        lifted = dot_n(turned, lift_weight[...]) + bias
        kind = rows % 64 // side
        there = jnp.where(kind == 0, south, jnp.where(kind == 1, north, jnp.where(
            kind == 2, east, west)))
        lifted = jnp.where(there >= 0, lifted, 0.0)
        halo_lifted[pair] = lifted.astype(BF).astype(F32)

    def lift(step, position):
        sigma = sigma_of(position)
        in_scale = lax.rsqrt(sigma * sigma + 1.0)
        frame = position + 1
        if frame < frame_count:
            value = frames_f32[frame]
        elif frame < reach:
            value = next_low[step, frame - frame_count].astype(F32)
            if frame == frame_count:
                entering = sigma_own[frame_count - 1 : frame_count] * noise[step]
                value = jnp.where(is_last, entering, value)
                frames_f32[frame] = value
        else:
            value = second_low[step].astype(F32)
            entering = sigma_next[frame_count - 1 : frame_count] * noise[step]
            value = jnp.where(is_tail, entering, value)
        scaled[position % 2, :fields] = value * in_scale
        turned = scaled[position % 2].T.astype(BF)
        lifted = dot_n(turned, lift_weight[...]) + jnp.log(sigma) * level_embed[...]
        lifted = lifted.astype(BF).astype(F32)
        pair, base = frame // 2, frame % 2 * 64
        south_row = halo_lifted[pair, base : base + side]
        north_row = halo_lifted[pair, base + side : base + 2 * side]
        tall = jnp.concatenate([north_row, lifted, south_row], axis=0)
        padded[position, :, width : 2 * width] = tall.astype(BF)
        east_col, west_col = base + 2 * side, base + 3 * side
        ends = 128 + base
        west_rows = [ends + 2 * side - 1] + [west_col + y for y in range(side)] + [ends + side - 1]
        east_rows = [ends + side] + [east_col + y for y in range(side)] + [ends]

        def spread(rows):
            return jnp.concatenate([
                jnp.broadcast_to(halo_lifted[pair, r : r + 1], (side, width)) for r in rows
            ], axis=0)

        total = (side + 2) * side
        along = lax.broadcasted_iota(jnp.int32, (total, 1), 0) % side
        from_west = jnp.where(along == 0, spread(west_rows), pltpu.roll(tall, 1, 0))
        padded[position, :, :width] = from_west.astype(BF)
        from_east = jnp.where(along == side - 1, spread(east_rows), pltpu.roll(tall, total - 1, 0))
        padded[position, :, 2 * width :] = from_east.astype(BF)

    def convolve(index):
        frames = pl.ds(2 * index, 2)
        total = None
        for offset in range(9):
            down, right = offset // 3, offset % 3
            window = padded[frames, down * side : down * side + cells, right * width : (right + 1) * width]
            product = dot_t(window.reshape(2 * cells, width), conv_weight[offset])
            total = product if total is None else total + product
        centre = padded[frames, side : side + cells, width : 2 * width].reshape(2 * cells, width)
        result = (centre.astype(F32) + total / (1.0 + jnp.exp(-total))).astype(BF)
        hidden[frames] = result.reshape(2, cells, width)
        widened = result.astype(F32)
        mean = jnp.mean(widened * widened, axis=1, keepdims=True)
        norm = (widened * lax.rsqrt(mean + 1e-06) * norm_gain[...]).astype(BF)
        memory[frames] = dot_t(norm, memory_weight[...]).astype(BF).reshape(2, cells, 2 * width)
        normed[frames] = norm.reshape(2, cells, width)

    rows_at_once = 128

    def attend(chunk):
        begin = pl.multiple_of(chunk * rows_at_once, rows_at_once)
        here = pl.ds(begin, rows_at_once)
        def partial(i, j):
            product = queries[i, here] * memory[j, here, :width]
            total = product[:, :128]
            for start in range(128, width, 128):
                total = total + product[:, start : start + 128]
            return total

        def score_block(first):
            pieces = [partial(c % frame_count, first + c // frame_count) for c in range(pairs)]
            return dot_n(jnp.concatenate(pieces, axis=1), head_sum[...]) * head_size ** (-0.5)

        near = score_block(0)
        far = jnp.where(is_last, -jnp.inf, score_block(frame_count))
        most = jnp.maximum(near, far)
        most = jnp.maximum(most, pltpu.roll(most, 64, 1))
        most = jnp.maximum(most, pltpu.roll(most, 32, 1))
        near = jnp.exp(near - most)
        far = jnp.exp(far - most)
        total = near + far
        total = total + pltpu.roll(total, 64, 1)
        total = total + pltpu.roll(total, 32, 1)
        inverse = 1.0 / total
        near = (near * inverse).astype(BF)
        far = (far * inverse).astype(BF)
        for i in range(frame_count):
            context = None
            columns = slice(i * frame_count * 128, (i + 1) * frame_count * 128)
            for block, weight in enumerate((near, far)):
                spread = dot_n(weight, head_spread[:, columns]).astype(BF)
                some = None
                for at in range(frame_count):
                    wide = spread[:, at * 128 : (at + 1) * 128]
                    values = memory[block * frame_count + at, here, width:]
                    term = jnp.concatenate([wide] * (width // 128), axis=1) * values
                    some = term if some is None else some + term
                some = some.astype(F32)
                context = some if context is None else context + some
            refined = hidden[i, here].astype(F32) + dot_t(context.astype(BF), attend_out[...])
            projected = dot_t(decode_weight[...], refined.astype(BF))
            sigma = sigma_own[i : i + 1, :rows_at_once]
            spread = sigma * sigma + 1.0
            frame = frames_f32[i + 1, :, here]
            denoised = (1.0 / spread) * frame + (sigma * lax.rsqrt(spread)) * projected
            change = (deltas[i][:, :rows_at_once] - sigma) / sigma
            frames_f32[i, :, here] = frame + change * (frame - denoised)

    for step in range(steps):
        prepare(step)
        if step == 0:
            reached = sum(
                jnp.where(jnp.logical_and(group + away >= 0, group + away < groups), tiles, 0)
                for away in (-2, -1, 1, 2)
            )
            pl.semaphore_wait(barrier, tiles - 1 + reached)
        send(step, step == 0)
        if step == 0:
            query_weight[...] = dot_n(order, query_raw[...]).astype(BF)
            memory_weight[:width] = dot_n(order, memory_raw[:width]).astype(BF)
            memory_weight[width:] = dot_n(order, memory_raw[width:]).astype(BF)
            attend_out[...] = dot_t(attend_raw[...], order).astype(BF)
        half = frame_count // 2
        arrive_own(step, step == 0)
        for pair in range(half):
            halo_of(step, pair)
        for position in range(frame_count - 1):
            lift(step, position)
        if step == 0:
            load.wait()
        lax.fori_loop(0, half // 2, lambda index, c: (convolve(index), c)[1], 0)
        arrive_next(step, step == 0)
        for pair in range(half, frame_count):
            halo_of(step, pair)
        for position in range(frame_count - 1, reach - 1):
            lift(step, position)
        arrive_second(step)
        halo_of(step, frame_count)
        lift(step, reach - 1)
        lax.fori_loop(half // 2, frame_count, lambda index, c: (convolve(index), c)[1], 0)
        for i in range(frame_count):
            queries[i] = dot_t(normed[i], query_weight[...]).astype(BF)
        lax.fori_loop(0, cells // rows_at_once, lambda chunk, c: (attend(chunk), c)[1], 0)
        sent(step, step == 0)
    for half in range(halves):
        across = slice(half * 128, (half + 1) * 128)
        for i in range(frame_count):
            out[pl.ds(i * halves * fields + half, fields, halves), :] = frames_f32[i, :, across]


def shards(groups, tiles, queue_state, fresh_noise, plan, levels, neighbours, in_weight, level_embed,
           conv_weight, norm_gain, query_weight, memory_weight, attend_out, decode_weight):
    frames, fields, _, cells = queue_state.shape
    steps = fresh_noise.shape[0]
    width = in_weight.shape[0]
    side = math.isqrt(cells)
    reach = 2 * frames
    vmem = pl.BlockSpec(memory_space=pltpu.VMEM)
    smem = pl.BlockSpec(memory_space=pltpu.SMEM)
    dma = pltpu.SemaphoreType.DMA
    result = pl.pallas_call(
        functools.partial(kernel, groups, tiles),
        out_shape=jax.ShapeDtypeStruct((frames * fields * cells // 128, 128), F32),
        in_specs=[smem] * 3 + [vmem] * 4 + [pl.BlockSpec(memory_space=pl.ANY)] + [vmem] * 5,
        out_specs=vmem,
        scratch_shapes=[
            pltpu.VMEM(conv_weight.shape, BF),
            pltpu.VMEM(query_weight.shape, BF),
            pltpu.VMEM(memory_weight.shape, BF),
            pltpu.VMEM(attend_out.shape, BF),
            pltpu.VMEM((steps, fields, cells), F32),
            pltpu.VMEM((frames + 1, fields, cells), F32),
            pltpu.VMEM((steps, frames, fields, cells), BF),
            pltpu.VMEM((steps, frames, fields, cells), BF),
            pltpu.VMEM((steps, fields, cells), BF),
            pltpu.VMEM((tiles, frames // 2, fields, 128), BF),
            pltpu.VMEM((tiles, frames // 2, fields, 128), BF),
            pltpu.VMEM((tiles, frames // 2, fields, 128), BF),
            pltpu.VMEM((tiles, frames // 2, fields, 128), BF),
            pltpu.VMEM((tiles, fields, 128), BF),
            pltpu.VMEM((tiles, fields, 128), BF),
            pltpu.VMEM((tiles, steps, fields, 128), BF),
            pltpu.VMEM((8, 256), F32),
            pltpu.VMEM((8, 256), F32),
            pltpu.VMEM((128, width), BF),
            pltpu.VMEM((frames * frames * 128, 128), BF),
            pltpu.VMEM((128, frames * frames * 128), BF),
            pltpu.VMEM((2, cells, 128), BF),
            pltpu.VMEM((2, 128, cells), F32),
            pltpu.VMEM((frames + 1, 128, 256), F32),
            pltpu.VMEM((frames + 1, 256, width), F32),
            pltpu.VMEM((reach, (side + 2) * side, 3 * width), BF),
            pltpu.VMEM((reach, cells, width), BF),
            pltpu.VMEM((reach, cells, width), BF),
            pltpu.VMEM((frames, cells, width), BF),
            pltpu.VMEM((reach, cells, 2 * width), BF),
            dma,
            dma((steps, 5, max(tiles, 3))),
            dma((steps, tiles)),
            dma((steps, tiles)),
            dma((steps, tiles)),
            dma((tiles,)),
            dma((steps, 3)),
        ],
        compiler_params=pltpu.CompilerParams(
            collective_id=0, has_side_effects=True, vmem_limit_bytes=56 * 1024 * 1024
        ),
    )(
        levels, plan, neighbours, queue_state.reshape(-1, 128),
        fresh_noise, in_weight.T, level_embed.reshape(1, width),
        conv_weight, norm_gain.reshape(1, width), query_weight, memory_weight, attend_out,
        decode_weight,
    )
    return result.reshape(queue_state.shape)


def solution(mesh):
    body = functools.partial(shards, mesh.shape["noise"], mesh.shape["tile"])
    in_specs = (
        P("noise", None, "tile", None), P(None, None, "tile", None), P(), P("noise"),
    ) + (P(),) * 9
    return jax.shard_map(
        body, mesh=mesh, in_specs=in_specs, out_specs=P("noise", None, "tile", None), check_vma=False
    )
```

```python
import functools
import math

import jax
import jax.numpy as jnp
from jax import lax
from jax.experimental import pallas as pl
from jax.experimental.pallas import tpu as pltpu
from jax.sharding import PartitionSpec as P

HEADS = 8
MESH = pl.DeviceIdType.MESH
BF = jnp.bfloat16
F32 = jnp.float32


def dot_t(left, right):
    return lax.dot_general(left, right, (((1,), (1,)), ((), ())), preferred_element_type=F32)


def dot_n(left, right):
    return lax.dot_general(left, right, (((1,), (0,)), ((), ())), preferred_element_type=F32)


def kernel(
    groups, tiles, levels, plan, neighbours, queue, noise_rows, in_weight, level_embed, conv_hbm,
    norm_gain, query_raw, memory_raw, attend_raw, decode_weight, out,
    conv_weight, query_weight, memory_weight, attend_out, noise, frames_f32, own_low, next_low, second_low, own_edges, own_edges_1, next_edges, next_edges_1,
    second_edges, second_edges_1, noise_edges,
    sigma_own, sigma_next, lift_weight, head_sum, head_spread, pick, scaled, halo, halo_lifted,
    padded, hidden, normed, queries, memory, load_sem,
    send_sems, own_sems, next_sems, second_sems, noise_sems, frame_sems,
):
    frame_count, fields, cells = padded.shape[0] // 2, in_weight.shape[0], hidden.shape[1]
    steps = own_low.shape[0]
    width = in_weight.shape[1]
    halves = cells // 128
    side = math.isqrt(cells)
    head_size = width // HEADS
    reach = 2 * frame_count
    own_edges = (own_edges, own_edges_1)
    next_edges = (next_edges, next_edges_1)
    second_edges = (second_edges, second_edges_1)
    me = lax.axis_index("tile")
    group = lax.axis_index("noise")
    is_last = group == groups - 1
    is_tail = group == groups - 2

    def tile_at(k):
        return lax.rem(me + k, tiles)

    load = pltpu.make_async_copy(conv_hbm, conv_weight, load_sem)
    load.start()
    barrier = pltpu.get_barrier_semaphore()
    for k in range(1, tiles):
        pl.semaphore_signal(
            barrier, 1, device_id={"noise": group, "tile": tile_at(k)}, device_id_type=MESH
        )
    for away in (-2, -1, 1, 2):
        @pl.when(jnp.logical_and(group + away >= 0, group + away < groups))
        def _():
            for k in range(tiles):
                pl.semaphore_signal(
                    barrier, 1, device_id={"noise": group + away, "tile": tile_at(k)},
                    device_id_type=MESH,
                )

    row = lax.broadcasted_iota(jnp.int32, (cells, 128), 0)
    lane = lax.broadcasted_iota(jnp.int32, (cells, 128), 1)
    part = lane % 64 // side
    spot = lane % side
    target = jnp.where(
        part == 0, spot, jnp.where(part == 1, (side - 1) * side + spot, jnp.where(
            part == 2, spot * side, spot * side + side - 1)))
    hit = row == target
    pick[0] = jnp.where(jnp.logical_and(hit, lane < 64), 1.0, 0.0).astype(BF)
    pick[1] = jnp.where(jnp.logical_and(hit, lane >= 64), 1.0, 0.0).astype(BF)
    pairs = frame_count * frame_count
    source = lax.broadcasted_iota(jnp.int32, (pairs * 128, 128), 0)
    target = lax.broadcasted_iota(jnp.int32, (pairs * 128, 128), 1)
    low = source % 128
    combo = source // 128
    head_sum[...] = jnp.where(target == combo * HEADS + low % HEADS, 1.0, 0.0).astype(BF)
    source = lax.broadcasted_iota(jnp.int32, (128, pairs * 128), 0)
    target = lax.broadcasted_iota(jnp.int32, (128, pairs * 128), 1)
    place = target // 128
    combo = place % frame_count * frame_count + place // frame_count
    head_spread[...] = jnp.where(source == combo * HEADS + target % HEADS, 1.0, 0.0).astype(BF)
    source = lax.broadcasted_iota(jnp.int32, (width, width), 1)
    target = lax.broadcasted_iota(jnp.int32, (width, width), 0)
    order = jnp.where(
        source == target % HEADS * head_size + target // HEADS, 1.0, 0.0
    ).astype(BF)
    lift_weight[...] = jnp.zeros_like(lift_weight)
    lift_weight[:fields] = in_weight[...]
    scaled[...] = jnp.zeros_like(scaled)
    halo[...] = jnp.zeros_like(halo)
    sigma_own[...] = jnp.ones_like(sigma_own)
    deltas = []
    for i in range(frame_count):
        sigma_own[i : i + 1] = jnp.full((1, 256), plan[levels[i]], F32)
        deltas.append(jnp.full((1, 256), plan[levels[i] + 1], F32))

    @pl.when(is_last)
    def _():
        sigma_next[...] = jnp.ones_like(sigma_next)
        next_low[...] = jnp.zeros_like(next_low)
        for edges in next_edges:
            edges[...] = jnp.zeros_like(edges)

    @pl.when(group >= groups - 2)
    def _():
        second_low[...] = jnp.zeros_like(second_low)
        for edges in second_edges:
            edges[...] = jnp.zeros_like(edges)

    for half in range(halves):
        across = slice(half * 128, (half + 1) * 128)
        for i in range(frame_count):
            frames_f32[i, :, across] = queue[pl.ds(i * halves * fields + half, fields, halves), :]
        for i in range(steps):
            noise[i, :, across] = noise_rows[i, :, 0, across]
    for s in range(steps):
        both = dot_n(noise[s].astype(BF), pick[0] + pick[1])
        noise_edges[me, s] = both.astype(BF)

    west, east = neighbours[me, 0], neighbours[me, 1]
    north, south = neighbours[me, 2], neighbours[me, 3]
    north_in, south_in = jnp.maximum(north, 0), jnp.maximum(south, 0)
    north_west, north_east = neighbours[north_in, 0], neighbours[north_in, 1]
    south_west, south_east = neighbours[south_in, 0], neighbours[south_in, 1]
    around = [jnp.maximum(t, 0) for t in (south, north, east, west)]
    corner = [jnp.maximum(t, 0) for t in (south_east, south_west, north_east, north_west)]

    def copy(source, target_ref, send, recv, where):
        return pltpu.make_async_remote_copy(
            src_ref=source, dst_ref=target_ref, send_sem=send, recv_sem=recv,
            device_id=where, device_id_type=MESH,
        )

    def to_own(step, k, sender):
        return copy(
            own_edges[step].at[sender], own_edges[step].at[sender], send_sems.at[step, 0, k],
            own_sems.at[step, sender], {"noise": group, "tile": tile_at(k)},
        )

    def to_noise(k, sender):
        return copy(
            noise_edges.at[sender], noise_edges.at[sender], send_sems.at[0, 3, k],
            noise_sems.at[sender], {"noise": group, "tile": tile_at(k)},
        )

    def to_next(step, k, sender):
        return copy(
            own_edges[step].at[sender], next_edges[step].at[sender], send_sems.at[step, 1, k],
            next_sems.at[step, sender], {"noise": group - 1, "tile": tile_at(k)},
        )

    def to_second(step, k, sender):
        return copy(
            own_edges[step].at[sender, 0], second_edges[step].at[sender], send_sems.at[step, 2, k],
            second_sems.at[step, sender], {"noise": group - 2, "tile": tile_at(k)},
        )

    def frame_copy(step):
        return copy(
            own_low.at[step], next_low.at[step], send_sems.at[step, 4, 0], frame_sems.at[step, 0],
            {"noise": group - 1, "tile": me},
        )

    def front_copy(step):
        return copy(
            own_low.at[step, 0], second_low.at[step], send_sems.at[step, 4, 1],
            frame_sems.at[step, 1], {"noise": group - 2, "tile": me},
        )

    def sigma_copy():
        return copy(
            sigma_own, sigma_next, send_sems.at[0, 4, 2], frame_sems.at[0, 2],
            {"noise": group - 1, "tile": me},
        )

    def prepare(step):
        for f in range(frame_count):
            own_low[step, f] = frames_f32[f].astype(BF)
        for pair in range(frame_count // 2):
            edges = dot_n(own_low[step, 2 * pair], pick[0]) + dot_n(
                own_low[step, 2 * pair + 1], pick[1]
            )
            own_edges[step][me, pair] = edges.astype(BF)

    def send(step, first):
        for k in range(1, tiles):
            to_own(step, k, me).start()
            if first:
                to_noise(k, me).start()

        @pl.when(group >= 1)
        def _():
            if first:
                sigma_copy().start()
            frame_copy(step).start()
            for k in range(1, tiles):
                to_next(step, k, me).start()

        @pl.when(group >= 2)
        def _():
            front_copy(step).start()
            for k in range(1, tiles):
                to_second(step, k, me).start()

    def arrive_own(step, first):
        for k in range(1, tiles):
            to_own(step, k, tile_at(k)).wait_recv()
            if first:
                to_noise(k, tile_at(k)).wait_recv()

    def arrive_next(step, first):
        @pl.when(group < groups - 1)
        def _():
            if first:
                sigma_copy().wait_recv()
            frame_copy(step).wait_recv()
            for k in range(1, tiles):
                to_next(step, k, tile_at(k)).wait_recv()

    def arrive_second(step):
        @pl.when(group < groups - 2)
        def _():
            front_copy(step).wait_recv()
            for k in range(1, tiles):
                to_second(step, k, tile_at(k)).wait_recv()

    def sent(step, first):
        for k in range(1, tiles):
            to_own(step, k, me).wait_send()
            if first:
                to_noise(k, me).wait_send()

        @pl.when(group >= 1)
        def _():
            if first:
                sigma_copy().wait_send()
            frame_copy(step).wait_send()
            for k in range(1, tiles):
                to_next(step, k, me).wait_send()

        @pl.when(group >= 2)
        def _():
            front_copy(step).wait_send()
            for k in range(1, tiles):
                to_second(step, k, me).wait_send()

    def sigma_of(position):
        if position < frame_count:
            return sigma_own[position : position + 1]
        return sigma_next[position - frame_count : position - frame_count + 1]

    lane1 = lax.broadcasted_iota(jnp.int32, (1, 128), 1)
    slot = lane1 % 64 // side

    def halo_of(step, pair):
        if pair < frame_count // 2:
            load = lambda t: own_edges[step][t, pair].astype(F32)
        elif pair < frame_count:
            load = lambda t: next_edges[step][t, pair - frame_count // 2].astype(F32)
        else:
            load = lambda t: second_edges[step][t].astype(F32)
        fresh = None
        if pair == frame_count // 2:
            take, scale = jnp.logical_and(is_last, lane1 < 64), sigma_own
            fresh = True
        elif pair == frame_count:
            take, scale = jnp.logical_and(is_tail, lane1 < 64), sigma_next
            fresh = True

        def load_all(t):
            value = load(t)
            if fresh:
                fresh_value = noise_edges[t, step].astype(F32) * scale[
                    frame_count - 1 : frame_count, :128
                ]
                value = jnp.where(take, fresh_value, value)
            return value

        parts = [load_all(t) for t in around]
        middle = jnp.where(slot == 0, parts[0], jnp.where(
            slot == 1, parts[1], jnp.where(slot == 2, parts[2], parts[3])))
        parts = [load_all(t) for t in corner]
        place = lane1 % 64
        ends = jnp.where(place == 0, parts[0], jnp.where(
            place == side - 1, parts[1], jnp.where(place == side, parts[2], parts[3])))
        low = sigma_of(max(2 * pair - 1, 0))
        high = sigma_of(min(2 * pair, reach - 1))
        sigma = jnp.where(lane1 < 64, low[:, :128], high[:, :128])
        in_scale = lax.rsqrt(sigma * sigma + 1.0)
        halo[pair, :fields, :128] = middle * in_scale
        halo[pair, :fields, 128:] = ends * in_scale
        turned = halo[pair].T.astype(BF)
        rows = lax.broadcasted_iota(jnp.int32, (256, 1), 0) % 128
        bias = jnp.where(rows < 64, jnp.log(low), jnp.log(high)) * level_embed[...]
        lifted = dot_n(turned, lift_weight[...]) + bias
        kind = rows % 64 // side
        there = jnp.where(kind == 0, south, jnp.where(kind == 1, north, jnp.where(
            kind == 2, east, west)))
        lifted = jnp.where(there >= 0, lifted, 0.0)
        halo_lifted[pair] = lifted.astype(BF).astype(F32)

    def lift(step, position):
        sigma = sigma_of(position)
        in_scale = lax.rsqrt(sigma * sigma + 1.0)
        frame = position + 1
        if frame < frame_count:
            value = frames_f32[frame]
        elif frame < reach:
            value = next_low[step, frame - frame_count].astype(F32)
            if frame == frame_count:
                entering = sigma_own[frame_count - 1 : frame_count] * noise[step]
                value = jnp.where(is_last, entering, value)
                frames_f32[frame] = value
        else:
            value = second_low[step].astype(F32)
            entering = sigma_next[frame_count - 1 : frame_count] * noise[step]
            value = jnp.where(is_tail, entering, value)
        scaled[position % 2, :fields] = value * in_scale
        turned = scaled[position % 2].T.astype(BF)
        lifted = dot_n(turned, lift_weight[...]) + jnp.log(sigma) * level_embed[...]
        lifted = lifted.astype(BF).astype(F32)
        pair, base = frame // 2, frame % 2 * 64
        south_row = halo_lifted[pair, base : base + side]
        north_row = halo_lifted[pair, base + side : base + 2 * side]
        tall = jnp.concatenate([north_row, lifted, south_row], axis=0)
        padded[position, :, width : 2 * width] = tall.astype(BF)
        east_col, west_col = base + 2 * side, base + 3 * side
        ends = 128 + base
        west_rows = [ends + 2 * side - 1] + [west_col + y for y in range(side)] + [ends + side - 1]
        east_rows = [ends + side] + [east_col + y for y in range(side)] + [ends]

        def spread(rows):
            return jnp.concatenate([
                jnp.broadcast_to(halo_lifted[pair, r : r + 1], (side, width)) for r in rows
            ], axis=0)

        total = (side + 2) * side
        along = lax.broadcasted_iota(jnp.int32, (total, 1), 0) % side
        from_west = jnp.where(along == 0, spread(west_rows), pltpu.roll(tall, 1, 0))
        padded[position, :, :width] = from_west.astype(BF)
        from_east = jnp.where(along == side - 1, spread(east_rows), pltpu.roll(tall, total - 1, 0))
        padded[position, :, 2 * width :] = from_east.astype(BF)

    def convolve(index):
        frames = pl.ds(2 * index, 2)
        total = None
        for offset in range(9):
            down, right = offset // 3, offset % 3
            window = padded[frames, down * side : down * side + cells, right * width : (right + 1) * width]
            product = dot_t(window.reshape(2 * cells, width), conv_weight[offset])
            total = product if total is None else total + product
        centre = padded[frames, side : side + cells, width : 2 * width].reshape(2 * cells, width)
        result = (centre.astype(F32) + total / (1.0 + jnp.exp(-total))).astype(BF)
        hidden[frames] = result.reshape(2, cells, width)
        widened = result.astype(F32)
        mean = jnp.mean(widened * widened, axis=1, keepdims=True)
        norm = (widened * lax.rsqrt(mean + 1e-06) * norm_gain[...]).astype(BF)
        memory[frames] = dot_t(norm, memory_weight[...]).astype(BF).reshape(2, cells, 2 * width)
        normed[frames] = norm.reshape(2, cells, width)

    rows_at_once = cells

    def attend(chunk):
        begin = pl.multiple_of(chunk * rows_at_once, rows_at_once)
        here = pl.ds(begin, rows_at_once)
        def partial(i, j):
            product = queries[i, here] * memory[j, here, :width]
            total = product[:, :128]
            for start in range(128, width, 128):
                total = total + product[:, start : start + 128]
            return total

        def score_block(first):
            pieces = [partial(c % frame_count, first + c // frame_count) for c in range(pairs)]
            return dot_n(jnp.concatenate(pieces, axis=1), head_sum[...]) * head_size ** (-0.5)

        near = score_block(0)
        far = jnp.where(is_last, -jnp.inf, score_block(frame_count))
        most = jnp.maximum(near, far)
        most = jnp.maximum(most, pltpu.roll(most, 64, 1))
        most = jnp.maximum(most, pltpu.roll(most, 32, 1))
        near = jnp.exp(near - most)
        far = jnp.exp(far - most)
        total = near + far
        total = total + pltpu.roll(total, 64, 1)
        total = total + pltpu.roll(total, 32, 1)
        inverse = 1.0 / total
        near = (near * inverse).astype(BF)
        far = (far * inverse).astype(BF)
        for i in range(frame_count):
            context = None
            columns = slice(i * frame_count * 128, (i + 1) * frame_count * 128)
            for block, weight in enumerate((near, far)):
                spread = dot_n(weight, head_spread[:, columns]).astype(BF)
                some = None
                for at in range(frame_count):
                    wide = spread[:, at * 128 : (at + 1) * 128]
                    values = memory[block * frame_count + at, here, width:]
                    term = jnp.concatenate([wide] * (width // 128), axis=1) * values
                    some = term if some is None else some + term
                some = some.astype(F32)
                context = some if context is None else context + some
            refined = hidden[i, here].astype(F32) + dot_t(context.astype(BF), attend_out[...])
            projected = dot_t(decode_weight[...], refined.astype(BF))
            sigma = sigma_own[i : i + 1, :rows_at_once]
            spread = sigma * sigma + 1.0
            frame = frames_f32[i + 1, :, here]
            denoised = (1.0 / spread) * frame + (sigma * lax.rsqrt(spread)) * projected
            change = (deltas[i][:, :rows_at_once] - sigma) / sigma
            frames_f32[i, :, here] = frame + change * (frame - denoised)

    for step in range(steps):
        prepare(step)
        if step == 0:
            reached = sum(
                jnp.where(jnp.logical_and(group + away >= 0, group + away < groups), tiles, 0)
                for away in (-2, -1, 1, 2)
            )
            pl.semaphore_wait(barrier, tiles - 1 + reached)
        send(step, step == 0)
        if step == 0:
            query_weight[...] = dot_n(order, query_raw[...]).astype(BF)
            memory_weight[:width] = dot_n(order, memory_raw[:width]).astype(BF)
            memory_weight[width:] = dot_n(order, memory_raw[width:]).astype(BF)
            attend_out[...] = dot_t(attend_raw[...], order).astype(BF)
        half = frame_count // 2
        arrive_own(step, step == 0)
        for pair in range(half):
            halo_of(step, pair)
        for position in range(frame_count - 1):
            lift(step, position)
        if step == 0:
            load.wait()
        lax.fori_loop(0, half // 2, lambda index, c: (convolve(index), c)[1], 0)
        arrive_next(step, step == 0)
        for pair in range(half, frame_count):
            halo_of(step, pair)
        for position in range(frame_count - 1, reach - 1):
            lift(step, position)
        arrive_second(step)
        halo_of(step, frame_count)
        lift(step, reach - 1)
        lax.fori_loop(half // 2, frame_count, lambda index, c: (convolve(index), c)[1], 0)
        for i in range(frame_count):
            queries[i] = dot_t(normed[i], query_weight[...]).astype(BF)
        lax.fori_loop(0, cells // rows_at_once, lambda chunk, c: (attend(chunk), c)[1], 0)
        sent(step, step == 0)
    for half in range(halves):
        across = slice(half * 128, (half + 1) * 128)
        for i in range(frame_count):
            out[pl.ds(i * halves * fields + half, fields, halves), :] = frames_f32[i, :, across]


def shards(groups, tiles, queue_state, fresh_noise, plan, levels, neighbours, in_weight, level_embed,
           conv_weight, norm_gain, query_weight, memory_weight, attend_out, decode_weight):
    frames, fields, _, cells = queue_state.shape
    steps = fresh_noise.shape[0]
    width = in_weight.shape[0]
    side = math.isqrt(cells)
    reach = 2 * frames
    vmem = pl.BlockSpec(memory_space=pltpu.VMEM)
    smem = pl.BlockSpec(memory_space=pltpu.SMEM)
    dma = pltpu.SemaphoreType.DMA
    result = pl.pallas_call(
        functools.partial(kernel, groups, tiles),
        out_shape=jax.ShapeDtypeStruct((frames * fields * cells // 128, 128), F32),
        in_specs=[smem] * 3 + [vmem] * 4 + [pl.BlockSpec(memory_space=pl.ANY)] + [vmem] * 5,
        out_specs=vmem,
        scratch_shapes=[
            pltpu.VMEM(conv_weight.shape, BF),
            pltpu.VMEM(query_weight.shape, BF),
            pltpu.VMEM(memory_weight.shape, BF),
            pltpu.VMEM(attend_out.shape, BF),
            pltpu.VMEM((steps, fields, cells), F32),
            pltpu.VMEM((frames + 1, fields, cells), F32),
            pltpu.VMEM((steps, frames, fields, cells), BF),
            pltpu.VMEM((steps, frames, fields, cells), BF),
            pltpu.VMEM((steps, fields, cells), BF),
            pltpu.VMEM((tiles, frames // 2, fields, 128), BF),
            pltpu.VMEM((tiles, frames // 2, fields, 128), BF),
            pltpu.VMEM((tiles, frames // 2, fields, 128), BF),
            pltpu.VMEM((tiles, frames // 2, fields, 128), BF),
            pltpu.VMEM((tiles, fields, 128), BF),
            pltpu.VMEM((tiles, fields, 128), BF),
            pltpu.VMEM((tiles, steps, fields, 128), BF),
            pltpu.VMEM((8, 256), F32),
            pltpu.VMEM((8, 256), F32),
            pltpu.VMEM((128, width), BF),
            pltpu.VMEM((frames * frames * 128, 128), BF),
            pltpu.VMEM((128, frames * frames * 128), BF),
            pltpu.VMEM((2, cells, 128), BF),
            pltpu.VMEM((2, 128, cells), F32),
            pltpu.VMEM((frames + 1, 128, 256), F32),
            pltpu.VMEM((frames + 1, 256, width), F32),
            pltpu.VMEM((reach, (side + 2) * side, 3 * width), BF),
            pltpu.VMEM((reach, cells, width), BF),
            pltpu.VMEM((reach, cells, width), BF),
            pltpu.VMEM((frames, cells, width), BF),
            pltpu.VMEM((reach, cells, 2 * width), BF),
            dma,
            dma((steps, 5, max(tiles, 3))),
            dma((steps, tiles)),
            dma((steps, tiles)),
            dma((steps, tiles)),
            dma((tiles,)),
            dma((steps, 3)),
        ],
        compiler_params=pltpu.CompilerParams(
            collective_id=0, has_side_effects=True, vmem_limit_bytes=56 * 1024 * 1024
        ),
    )(
        levels, plan, neighbours, queue_state.reshape(-1, 128),
        fresh_noise, in_weight.T, level_embed.reshape(1, width),
        conv_weight, norm_gain.reshape(1, width), query_weight, memory_weight, attend_out,
        decode_weight,
    )
    return result.reshape(queue_state.shape)


def solution(mesh):
    body = functools.partial(shards, mesh.shape["noise"], mesh.shape["tile"])
    in_specs = (
        P("noise", None, "tile", None), P(None, None, "tile", None), P(), P("noise"),
    ) + (P(),) * 9
    return jax.shard_map(
        body, mesh=mesh, in_specs=in_specs, out_specs=P("noise", None, "tile", None), check_vma=False
    )
```
